32 devices in a mesh: row: 8 (over z, y), col: 4 (over x, core).
Axes of the slice: x: 2, y: 2, z: 4, core: 2. Of those that a mesh axis runs over, the one named last changes fastest.
Arguments:
- paths_in: float32 [4096, 256], P(('row', 'col')), may hold values from 0.05 to 4
- dep_in: float32 [4096, 256], P(('row', 'col')), may hold values from 0 to 4
- levels: int32 [4096, 256], P(('row', 'col')), may hold values from 0 to 4, as said below
- tile_src: int32 [8, 4, 8, 4], P('row', 'col'), may hold values from 0 to 3, as said below
- pattern: int32 [8, 4, 8, 4, 128, 128], P('row', 'col'), may hold values from 0 to 1, as said below
Outputs:
- dependency: float32 [4096, 256], P(('row', 'col'))
The draws below stay inside these ranges and needn't reach their ends.
Inputs may be any that keep to these rules, and one draw needn't show every extreme that they name: The value 4 marks a vertex outside the window's levels for that source. A program may send only the non-zero entries of a level's rounded path counts or backward weights, together with their positions, in any encoding that loses nothing. `tile_src`: within one device the 4 source tiles of a destination tile row are distinct, and every source tile index appears in exactly 8 of the device's slots. `pattern`: each slot holds either an all-zero tile or a tile of independent 0/1 entries; a device has from 1 to 32 nonzero tiles, and some device has all its slots nonzero.
All inputs are finite; a program needn't handle non-finite values.
Results may differ from the reference program's by a relative error of at most 0.0016.
Values may be sent and summed in bfloat16 or wider, within the bound.
No kernel may reach another device: no remote copies, remote signals or barrier semaphores. Data moves between devices by JAX's collectives and lax.ppermute only.
A program may use at most 64 MiB of HBM per device.

```python
import math
import jax
import jax.numpy as jnp
from jax import lax

VERT_DEV = 128
SOURCES = 256
TILE = 128
BAND = 4
ROW_BLOCKS = 8
COL_BLOCKS = 4
DEST_TILES = 8
SRC_TILES = 4
VERTICES = 4096
N_ROW = 8
N_COL = 4


def band_sources(device_key):
    key_perm, key_shift = jax.random.split(device_key)
    source_perm = jax.random.permutation(key_perm, SRC_TILES)
    row_shift = jax.random.permutation(key_shift, DEST_TILES)
    slots = (row_shift[:, None] + jnp.arange(BAND)[None, :]) % SRC_TILES
    return source_perm[slots].astype(jnp.int32)


def draw_tile_src(key, part):
    device_keys = jax.random.split(jax.random.fold_in(key, 11), ROW_BLOCKS * COL_BLOCKS)
    chosen = jax.vmap(band_sources)(device_keys)
    return chosen.reshape(ROW_BLOCKS, COL_BLOCKS, DEST_TILES, BAND)


def shuffled(rank_key):
    return jax.random.permutation(rank_key, DEST_TILES * BAND)


def draw_pattern(key, part):
    devices = ROW_BLOCKS * COL_BLOCKS
    slots = DEST_TILES * BAND
    key_count, key_top, key_rank, key_bits = jax.random.split(jax.random.fold_in(key, 23), 4)
    raw_draw = jax.random.randint(key_count, (devices,), 1, slots + 1)
    live_count = jnp.maximum(raw_draw * raw_draw // slots, 1)
    busiest = jax.random.randint(key_top, (), 0, devices)
    live_count = jnp.where(jnp.arange(devices) == busiest, slots, live_count)
    slot_rank = jax.vmap(shuffled)(jax.random.split(key_rank, devices))
    live_slots = slot_rank < live_count[:, None]
    entries = jax.random.randint(key_bits, (devices, slots, TILE, TILE), 0, 8) == 0
    values = jnp.logical_and(entries, live_slots[:, :, None, None]).astype(jnp.int32)
    return values.reshape(ROW_BLOCKS, COL_BLOCKS, DEST_TILES, BAND, TILE, TILE)


def draw_levels(key, part):
    key_order, key_ticket = jax.random.split(jax.random.fold_in(key, 37))
    source_order = jax.random.permutation(key_order, SOURCES).astype(jnp.int32)
    exponent = source_order * 8 // SOURCES
    ticket = jax.random.randint(key_ticket, (VERTICES, SOURCES), 0, 1024)
    bound_sum = jnp.zeros_like(exponent)
    level_value = jnp.zeros((VERTICES, SOURCES), jnp.int32)
    for section in range(4):
        one_share = jnp.minimum(jnp.left_shift(jnp.ones_like(exponent), exponent + 2 * section), 205)
        bound_sum = bound_sum + one_share
        level_value = level_value + (ticket >= bound_sum[None, :]).astype(jnp.int32)
    return level_value


def block_levels(rng, shape, pieces, low, largest):
    def one(position, shards_of):
        steps = jax.random.uniform(jax.random.fold_in(jax.random.fold_in(rng, 6), position), (shards_of,), jnp.float32, low / len(pieces), largest / len(pieces))
        return jnp.repeat(jnp.exp(steps), shape[position] // shards_of).reshape((-1,) + (1,) * (len(shape) - position - 1))

    factor_of = one(*pieces[0])
    for cut in pieces[1:]:
        factor_of = factor_of * one(*cut)
    return factor_of


def setup_inputs(seed: int = 0) -> dict:
    keys = jax.random.split(jax.random.key(seed), 6)
    paths_in = jnp.clip(jnp.exp(math.log(4.0) - 4.3820266 * jax.random.uniform(keys[0], (VERTICES, SOURCES), jnp.float32) ** block_levels(keys[0], (VERTICES, SOURCES), ((0, 32),), -0.2, 0.2)), 0.05, 4.0)
    dep_in = jnp.clip(4.0 * jax.random.uniform(keys[1], (VERTICES, SOURCES), jnp.float32) ** block_levels(keys[1], (VERTICES, SOURCES), ((0, 32),), -0.2, 0.2), 0.0, 4.0)
    levels = draw_levels(jax.random.fold_in(keys[5], 71), 0)
    tile_src = draw_tile_src(jax.random.fold_in(keys[5], 71), 0)
    pattern = draw_pattern(jax.random.fold_in(keys[5], 71), 0)
    return dict(paths_in=paths_in, dep_in=dep_in, levels=levels, tile_src=tile_src, pattern=pattern)


def rounded(values):
    return lax.optimization_barrier(values.astype(jnp.bfloat16)).astype(jnp.float32)


def forward_apply(frontier, tile_src, pattern):
    vtiles = VERT_DEV // TILE
    blocked = frontier.reshape(N_ROW, N_COL * VERT_DEV, SOURCES)
    summed = jnp.zeros((N_ROW, N_COL, VERT_DEV, SOURCES), jnp.float32)

    def visit(device, summed):
        row_block = (device // N_COL).astype(jnp.int32)
        col_block = (device % N_COL).astype(jnp.int32)
        anchor = jnp.zeros((), jnp.int32)
        source_block = lax.dynamic_index_in_dim(blocked, row_block, 0, keepdims=False)
        source_block = source_block.reshape(N_COL * vtiles, TILE, SOURCES)
        source_ids = tile_src[row_block, col_block]
        tile_values = pattern[row_block, col_block].astype(jnp.float32)
        picked = source_block[source_ids]
        product = jnp.einsum("ibrj,ibjs->irs", tile_values, picked, precision=lax.Precision.HIGHEST)
        product = product.reshape(N_ROW, 1, VERT_DEV, SOURCES)
        current = lax.dynamic_slice(summed, (anchor, col_block, anchor, anchor), (N_ROW, 1, VERT_DEV, SOURCES))
        return lax.dynamic_update_slice(summed, current + product, (anchor, col_block, anchor, anchor))

    summed = lax.fori_loop(jnp.int32(0), jnp.int32(N_ROW * N_COL), visit, summed)
    return summed.reshape(N_ROW * N_COL * VERT_DEV, SOURCES)


def backward_apply(weight, tile_src, pattern):
    vtiles = VERT_DEV // TILE
    src_count = N_COL * vtiles
    blocked = weight.reshape(N_ROW, N_COL, VERT_DEV, SOURCES)
    summed = jnp.zeros((N_ROW, N_COL * VERT_DEV, SOURCES), jnp.float32)

    def visit(device, summed):
        row_block = (device // N_COL).astype(jnp.int32)
        col_block = (device % N_COL).astype(jnp.int32)
        anchor = jnp.zeros((), jnp.int32)
        dest_block = lax.dynamic_index_in_dim(blocked, col_block, 1, keepdims=False)
        dest_block = dest_block.reshape(N_ROW * vtiles, TILE, SOURCES)
        source_ids = tile_src[row_block, col_block]
        tile_values = pattern[row_block, col_block].astype(jnp.float32)
        spread = jnp.einsum("ibrj,irs->ibjs", tile_values, dest_block, precision=lax.Precision.HIGHEST)
        select = (source_ids[:, :, None] == jnp.arange(src_count, dtype=jnp.int32)[None, None, :]).astype(jnp.float32)
        product = jnp.einsum("ibt,ibjs->tjs", select, spread, precision=lax.Precision.HIGHEST)
        product = product.reshape(1, N_COL * VERT_DEV, SOURCES)
        current = lax.dynamic_slice(summed, (row_block, anchor, anchor), (1, N_COL * VERT_DEV, SOURCES))
        return lax.dynamic_update_slice(summed, current + product, (row_block, anchor, anchor))

    summed = lax.fori_loop(jnp.int32(0), jnp.int32(N_ROW * N_COL), visit, summed)
    return summed.reshape(N_ROW * N_COL * VERT_DEV, SOURCES)


def reference(paths_in, dep_in, levels, tile_src, pattern):
    level_masks = [(levels == distance).astype(jnp.float32) for distance in range(4)]
    path_counts = [level_masks[0] * paths_in]
    for distance in range(1, 4):
        frontier = rounded(path_counts[-1])
        path_counts.append(level_masks[distance] * forward_apply(frontier, tile_src, pattern))
    weight = rounded(level_masks[3] * (1.0 + dep_in) / jnp.maximum(path_counts[3], 1.0))
    dependency = jnp.zeros(paths_in.shape, jnp.float32)
    for distance in (2, 1, 0):
        dependence = level_masks[distance] * path_counts[distance] * backward_apply(weight, tile_src, pattern)
        dependency = dependency + dependence
        if distance > 0:
            weight = rounded(level_masks[distance] * (1.0 + dependence) / jnp.maximum(path_counts[distance], 1.0))
    return dependency
```

```python
import jax
import jax.numpy as jnp
from jax import lax
from jax.sharding import PartitionSpec as P


def general_shards(paths_in, dep_in, levels, tile_src, pattern):
    vert_dev = paths_in.shape[0]
    tile_size = pattern.shape[-1]
    dest_tiles = tile_src.shape[2]
    band_slots = tile_src.shape[3]
    src_tiles = lax.axis_size("col") * vert_dev // tile_size
    per_source = dest_tiles * band_slots // src_tiles
    source_ids = tile_src[0, 0]
    tile_values = pattern[0, 0].astype(jnp.bfloat16)
    flat_ids = source_ids.reshape(-1)
    by_source = jnp.argsort(flat_ids, stable=True)
    back_values = tile_values.reshape(-1, tile_size, tile_size)[by_source]
    back_values = back_values.reshape(src_tiles, per_source, tile_size, tile_size)
    back_dest = (by_source // band_slots).reshape(src_tiles, per_source)

    def forward_terms(frontier):
        gathered = lax.all_gather(frontier, "col", axis=0, tiled=True)
        pieces = gathered.reshape(src_tiles, tile_size, gathered.shape[1])
        product = jnp.einsum(
            "ibrj,ibjs->irs", tile_values, pieces[source_ids], preferred_element_type=jnp.float32
        )
        terms = product.reshape(vert_dev * lax.axis_size("row"), product.shape[2])
        return lax.psum_scatter(terms, "row", scatter_dimension=0, tiled=True)

    def spread(weight):
        return lax.all_gather(weight, "row", axis=0, tiled=True)

    level_masks = [(levels == distance).astype(jnp.float32) for distance in range(4)]
    path_counts = [level_masks[0] * paths_in]
    for distance in (1, 2, 3):
        path_counts.append(
            level_masks[distance] * forward_terms(path_counts[-1].astype(jnp.bfloat16))
        )
    numerator = level_masks[3] * (1.0 + dep_in)
    spread_weight = spread((numerator / jnp.maximum(path_counts[3], 1.0)).astype(jnp.bfloat16))
    dependency = jnp.zeros(paths_in.shape, jnp.float32)
    for distance in (2, 1, 0):
        backward_pieces = spread_weight.reshape(dest_tiles, tile_size, spread_weight.shape[1])
        source_product = jnp.einsum(
            "tgrj,tgrs->tjs",
            back_values,
            backward_pieces[back_dest],
            preferred_element_type=jnp.float32,
        )
        source_product = source_product.reshape(
            vert_dev * lax.axis_size("col"), source_product.shape[2]
        )
        dependence = (
            level_masks[distance]
            * path_counts[distance]
            * lax.psum_scatter(source_product, "col", scatter_dimension=0, tiled=True)
        )
        dependency = dependency + dependence
        if distance > 0:
            weight = (
                level_masks[distance] * (1.0 + dependence) / jnp.maximum(path_counts[distance], 1.0)
            ).astype(jnp.bfloat16)
            spread_weight = spread(weight)
    return dependency


def partner(axis, bit):
    return [(i, i ^ bit) for i in range(lax.axis_size(axis))]


def swap(value, axis, bit):
    return lax.ppermute(value, axis, partner(axis, bit))


GROUP = 8
LAYERS = 4
STAGES = (("col", 1, 2), ("col", 2, 1), ("row", 1, 0))


def exchange(pieces):
    held = pieces
    for axis, bit, place in STAGES:
        keep, send = lax.index_in_dim(held, 0, place), lax.index_in_dim(held, 1, place)
        held = jnp.concatenate([keep, swap(send, axis, bit)], axis=place)
    return held


STEPS = 1625.0
LOWEST = 6.0


def coded(count):
    steps = jnp.clip((jnp.log2(count) + LOWEST) * STEPS + 1.5, 1.0, 65535.0)
    return jnp.where(count > 0.0, steps, 0.0).astype(jnp.int32).astype(jnp.uint16)


def decoded(code):
    steps = code.astype(jnp.int32).astype(jnp.float32)
    return jnp.where(steps > 0.0, jnp.exp2((steps - 1.0) * (1.0 / STEPS) - LOWEST), 0.0)


def split_shards(paths_in, dep_in, levels, tile_src, pattern):
    vert, sources = paths_in.shape
    share = sources // GROUP
    cols = lax.axis_size("col")
    tile = pattern.shape[-1]
    row, col = lax.axis_index("row"), lax.axis_index("col")
    layer, side = row >> 1, row & 1
    place = side * cols + col
    by_place = place ^ jnp.arange(GROUP)

    order = (((layer ^ jnp.arange(LAYERS)) << 1)[:, None] + (side ^ jnp.arange(2))[None, :]).reshape(-1)
    ids = tile_src[0, 0][order]
    slot = jnp.argmax(ids[:, None, :] == jnp.arange(cols)[None, :, None], axis=2)
    tiles = pattern[0, 0].reshape(-1, tile, tile).astype(jnp.bfloat16)
    own = tiles[order[:, None] * tile_src.shape[3] + slot]
    own = own.transpose(0, 2, 1, 3).reshape(LAYERS, 2, tile, cols * tile)
    flipped = jnp.flip(own, axis=1)

    by_x = swap(own, "col", 2)
    by_y = swap(flipped, "row", 1)
    by_core = swap(own, "col", 1)

    packed = levels.astype(jnp.float32) * 8.0 + jnp.where(
        levels == 0, paths_in, jnp.where(levels == 3, 1.0 + dep_in, 0.0)
    )
    pieces = packed.T.reshape(GROUP, share, vert)[by_place].reshape(2, 2, 2, share, vert)
    pieces = exchange(pieces).reshape(GROUP, share, vert)

    def by_vertex(values):
        return values.transpose(1, 0, 2).reshape(share, GROUP * vert)

    pieces = pieces.reshape(2, cols, share, vert)[:, col ^ jnp.arange(cols)]
    word = by_vertex(pieces.reshape(GROUP, share, vert))
    level = jnp.floor(word * 0.125)
    value = word - 8.0 * level
    masks = [(level == distance).astype(jnp.float32) for distance in range(4)]

    def placed(into, block, at_y, c):
        return lax.dynamic_update_slice(into, block[:, :, None], (0, at_y, c, 0, 0))

    cross_y = swap(by_x[:, :1], "row", 1)
    cross_x = swap(by_y[:, :1], "col", 2)
    empty = jnp.zeros((LAYERS, 2, cols, tile, cols * tile), jnp.bfloat16)
    near = placed(placed(empty, own, 0, col), by_core, 0, col ^ 1)
    near = placed(placed(near, by_x, 0, col ^ 2), swap(by_x, "col", 1), 0, col ^ 3)
    far = placed(placed(empty, by_y, 0, col), swap(by_y, "col", 1), 0, col ^ 1)
    far = placed(placed(far, cross_x, 0, col ^ 2), cross_y, 1, col ^ 2)
    far = placed(placed(far, swap(cross_x, "col", 1), 0, col ^ 3), swap(cross_y, "col", 1), 1, col ^ 3)
    span = GROUP * vert
    near, far = (half.reshape(LAYERS * span, cols * tile) for half in (near, far))

    def forward(front):
        front = front.astype(jnp.bfloat16)
        dims = (((1,), (1,)), ((), ()))
        return lax.dot_general(
            front[:, : cols * vert], near, dims, preferred_element_type=jnp.float32
        ) + lax.dot_general(front[:, cols * vert :], far, dims, preferred_element_type=jnp.float32)

    def backward(weights):
        dims = (((1,), (0,)), ((), ()))
        return jnp.concatenate(
            [
                lax.dot_general(weights, half, dims, preferred_element_type=jnp.float32)
                for half in (near, far)
            ],
            axis=1,
        )

    def across(value):
        return [swap(value[k], "row", 2 * k) for k in range(1, LAYERS)]

    counts = [masks[0] * value]
    for distance in (1, 2, 3):
        terms = forward(counts[-1])
        terms = [terms[:, k * span : (k + 1) * span] for k in range(LAYERS)]
        total = terms[0]
        for got in across([coded(t) for t in terms]):
            total = total + decoded(got)
        counts.append(masks[distance] * total)
    weight = (masks[3] * value / jnp.maximum(counts[3], 1.0)).astype(jnp.bfloat16)
    found = jnp.zeros_like(value)
    for distance in (2, 1, 0):
        gathered = jnp.concatenate([weight] + across([weight] * LAYERS), axis=1)
        back = backward(gathered)
        if distance > 0:
            delta = masks[distance] * counts[distance] * back
            found = found + delta
            weight = (
                masks[distance] * (1.0 + delta) / jnp.maximum(counts[distance], 1.0)
            ).astype(jnp.bfloat16)
        else:
            found = found + masks[0] * back

    found = found.reshape(share, 2, cols, vert).transpose(1, 2, 0, 3)[:, col ^ jnp.arange(cols)]
    home = exchange(found.reshape(2, 2, 2, share, vert)).reshape(GROUP, share, vert)[by_place]
    home = home.reshape(sources, vert).T
    return jnp.where(levels == 0, paths_in * home, home)


def solution(mesh):
    placed = (
        P(("row", "col"), None),
        P(("row", "col"), None),
        P(("row", "col"), None),
        P("row", "col", None, None),
        P("row", "col", None, None, None, None),
    )

    def shards(paths_in, dep_in, levels, tile_src, pattern):
        rows, cols = lax.axis_size("row"), lax.axis_size("col")
        fits = (
            rows == 2 * LAYERS
            and 2 * cols == GROUP
            and paths_in.shape[0] == pattern.shape[-1]
            and tile_src.shape[3] == cols
            and paths_in.shape[1] % GROUP == 0
        )
        chosen = split_shards if fits else general_shards
        return chosen(paths_in, dep_in, levels, tile_src, pattern)

    return jax.shard_map(
        shards, mesh=mesh, in_specs=placed, out_specs=P(("row", "col"), None), check_vma=False
    )
```

```python
import functools

import jax
import jax.numpy as jnp
from jax import lax
from jax.experimental import pallas as pl
from jax.experimental.pallas import tpu as pltpu
from jax.sharding import PartitionSpec as P


def general_shards(paths_in, dep_in, levels, tile_src, pattern):
    vert_dev = paths_in.shape[0]
    tile_size = pattern.shape[-1]
    dest_tiles = tile_src.shape[2]
    band_slots = tile_src.shape[3]
    src_tiles = lax.axis_size("col") * vert_dev // tile_size
    per_source = dest_tiles * band_slots // src_tiles
    source_ids = tile_src[0, 0]
    tile_values = pattern[0, 0].astype(jnp.bfloat16)
    flat_ids = source_ids.reshape(-1)
    by_source = jnp.argsort(flat_ids, stable=True)
    back_values = tile_values.reshape(-1, tile_size, tile_size)[by_source]
    back_values = back_values.reshape(src_tiles, per_source, tile_size, tile_size)
    back_dest = (by_source // band_slots).reshape(src_tiles, per_source)

    def forward_terms(frontier):
        gathered = lax.all_gather(frontier, "col", axis=0, tiled=True)
        pieces = gathered.reshape(src_tiles, tile_size, gathered.shape[1])
        product = jnp.einsum(
            "ibrj,ibjs->irs", tile_values, pieces[source_ids], preferred_element_type=jnp.float32
        )
        terms = product.reshape(vert_dev * lax.axis_size("row"), product.shape[2])
        return lax.psum_scatter(terms, "row", scatter_dimension=0, tiled=True)

    def spread(weight):
        return lax.all_gather(weight, "row", axis=0, tiled=True)

    level_masks = [(levels == distance).astype(jnp.float32) for distance in range(4)]
    path_counts = [level_masks[0] * paths_in]
    for distance in (1, 2, 3):
        path_counts.append(
            level_masks[distance] * forward_terms(path_counts[-1].astype(jnp.bfloat16))
        )
    numerator = level_masks[3] * (1.0 + dep_in)
    spread_weight = spread((numerator / jnp.maximum(path_counts[3], 1.0)).astype(jnp.bfloat16))
    dependency = jnp.zeros(paths_in.shape, jnp.float32)
    for distance in (2, 1, 0):
        backward_pieces = spread_weight.reshape(dest_tiles, tile_size, spread_weight.shape[1])
        source_product = jnp.einsum(
            "tgrj,tgrs->tjs",
            back_values,
            backward_pieces[back_dest],
            preferred_element_type=jnp.float32,
        )
        source_product = source_product.reshape(
            vert_dev * lax.axis_size("col"), source_product.shape[2]
        )
        dependence = (
            level_masks[distance]
            * path_counts[distance]
            * lax.psum_scatter(source_product, "col", scatter_dimension=0, tiled=True)
        )
        dependency = dependency + dependence
        if distance > 0:
            weight = (
                level_masks[distance] * (1.0 + dependence) / jnp.maximum(path_counts[distance], 1.0)
            ).astype(jnp.bfloat16)
            spread_weight = spread(weight)
    return dependency


def partner(axis, bit):
    return [(i, i ^ bit) for i in range(lax.axis_size(axis))]


def swap(value, axis, bit):
    return lax.ppermute(value, axis, partner(axis, bit))


def diagonal():
    cols = lax.axis_size("col")
    return [(i, i ^ cols ^ 2) for i in range(lax.axis_size("row") * cols)]


GROUP = 8
LAYERS = 4
LOWEST = 5
MANTISSA = 18
BYTE = 255


def coded(count):
    scaled = count * 2.0**LOWEST
    exponent = jnp.zeros_like(count)
    for bit in (32, 16, 8, 4, 2, 1):
        large = scaled >= 2.0**bit
        scaled = jnp.where(large, scaled * 2.0**-bit, scaled)
        exponent = exponent + jnp.where(large, float(bit), 0.0)
    mantissa = jnp.floor((scaled - 1.0) * 2.0**MANTISSA + 0.5)
    code = jnp.where(count > 0.0, exponent * 2.0**MANTISSA + mantissa, 0.0).astype(jnp.int32)
    *first, last = jnp.split(code, 4, axis=1)
    words = [part | (((last >> (8 * at)) & BYTE) << 24) for at, part in enumerate(first)]
    return jnp.concatenate(words, axis=1)


def decoded(words):
    words = jnp.split(words, 3, axis=1)
    last = sum(((word >> 24) & BYTE) << (8 * at) for at, word in enumerate(words))
    code = jnp.concatenate([word & (2**24 - 1) for word in words] + [last], axis=1)
    exponent = code >> MANTISSA
    mantissa = code & (2**MANTISSA - 1)
    count = mantissa.astype(jnp.float32) * 2.0 ** (-MANTISSA - LOWEST) + 2.0**-LOWEST
    for bit in (32, 16, 8, 4, 2, 1):
        count = jnp.where((exponent & bit) != 0, count * 2.0**bit, count)
    return jnp.where(code > 0, count, 0.0)


IN_VMEM = pl.BlockSpec(memory_space=pltpu.VMEM)
IN_SMEM = pl.BlockSpec(memory_space=pltpu.SMEM)


def pack_kernel(ids, pattern, *outs):
    cols = outs[0].shape[1]
    row = lax.axis_index("row")
    for y in range(2):
        for layer in range(LAYERS):
            i = row ^ (2 * layer + y)
            for t in range(cols):
                slot = jnp.int32(0)
                for e in range(1, cols):
                    slot = jnp.where(ids[e, i] == t, e, slot)
                outs[y][layer, t] = pattern[i * cols + slot].astype(jnp.float32).astype(jnp.bfloat16)


def packed_block(ids, pattern):
    cols, tile = ids.shape[0], pattern.shape[-1]
    half = jax.ShapeDtypeStruct((LAYERS, cols, tile, tile), jnp.bfloat16)
    return pl.pallas_call(
        pack_kernel,
        out_shape=[half] * 2,
        in_specs=[IN_SMEM, IN_VMEM],
        out_specs=[IN_VMEM] * 2,
        compiler_params=pltpu.CompilerParams(vmem_limit_bytes=8 * 1024 * 1024),
        name="pack",
    )(ids, pattern)


def inputs_kernel(paths_in, dep_in, levels, keep, send, words):
    level = levels[...]
    word = jnp.where(
        level == 0, -paths_in[...], jnp.where(level == 3, 1.0 + dep_in[...], 0.0)
    )
    word = jnp.where(level == 1, 0.5, jnp.where(level == 2, 0.25, word))
    words[...] = word.T
    share = keep.shape[-2]
    place = lax.axis_index("row") % 2 * lax.axis_size("col") + lax.axis_index("col")
    for out, core in ((keep, 0), (send, 1)):
        for at in range(GROUP // 2):
            rows = pl.multiple_of((place ^ (2 * at + core)) * share, share)
            out[at] = words[pl.ds(rows, share), :]


def packed_inputs(paths_in, dep_in, levels):
    vert, sources = paths_in.shape
    half = jax.ShapeDtypeStruct((GROUP // 2, sources // GROUP, vert), jnp.float32)
    return pl.pallas_call(
        inputs_kernel,
        out_shape=[half] * 2,
        in_specs=[IN_VMEM] * 3,
        out_specs=[IN_VMEM] * 2,
        scratch_shapes=[pltpu.VMEM((sources, vert), jnp.float32)],
        compiler_params=pltpu.CompilerParams(vmem_limit_bytes=4 * 1024 * 1024),
        name="inputs",
    )(paths_in, dep_in, levels)


def placed_kernel(*rest):
    pieces, word, front = rest[:-2], rest[-2], rest[-1]
    vert = pieces[0].shape[-1]
    col = lax.axis_index("col")
    for at in range(2 * len(pieces)):
        to = (at & 4) | ((at & 3) ^ col)
        piece = pieces[at // 2][at % 2]
        lanes = pl.ds(pl.multiple_of(to * vert, vert), vert)
        word[:, lanes] = piece
        front[:, lanes] = jnp.maximum(-piece, 0.0).astype(jnp.bfloat16)


def placed_inputs(pieces):
    _, share, vert = pieces[0].shape
    shape = (share, 2 * len(pieces) * vert)
    return pl.pallas_call(
        placed_kernel,
        out_shape=[jax.ShapeDtypeStruct(shape, kind) for kind in (jnp.float32, jnp.bfloat16)],
        in_specs=[IN_VMEM] * len(pieces),
        out_specs=[IN_VMEM] * 2,
        compiler_params=pltpu.CompilerParams(vmem_limit_bytes=4 * 1024 * 1024),
        name="placed",
    )(*pieces)


def rows_of(halves, layer):
    cols = halves[0].shape[1]
    return jnp.concatenate(
        [jnp.concatenate([half[layer, t] for t in range(cols)], axis=1) for half in halves], axis=0
    )


def first_kernel(base, front, *rest):
    outs = rest[-LAYERS:]
    start = rest[:LAYERS] if base else None
    halves = rest[LAYERS if base else 0 : -LAYERS]
    pairs = ((1, 2), (1, 3)) if base else tuple((at // 4, at % 4) for at in range(6))
    layers, cols, tile, _ = halves[0].shape
    wide = cols * tile
    col = lax.axis_index("col")
    for layer in range(layers):
        for flip in range(cols):
            terms = None
            for at, (side, c) in enumerate(pairs):
                if c == flip:
                    term = lax.dot_general(
                        front[:, side * wide : (side + 1) * wide],
                        rows_of(halves[2 * at : 2 * at + 2], layer),
                        (((1,), (1,)), ((), ())),
                        preferred_element_type=jnp.float32,
                    )
                    terms = term if terms is None else terms + term
            for y in range(2):
                lanes = pl.ds(pl.multiple_of((y * cols + (col ^ flip)) * tile, tile), tile)
                if terms is None:
                    outs[layer][:, lanes] = start[layer][:, lanes]
                    continue
                part = terms[:, y * tile : (y + 1) * tile]
                outs[layer][:, lanes] = part + start[layer][:, lanes] if base else part


def first_terms(front, base, halves):
    shape = jax.ShapeDtypeStruct(front.shape, jnp.float32)
    flops = 2 * front.shape[0] * len(halves) * halves[0].size
    return pl.pallas_call(
        functools.partial(first_kernel, bool(base)),
        out_shape=[shape] * LAYERS,
        in_specs=[IN_VMEM] * (1 + len(base) + len(halves)),
        out_specs=[IN_VMEM] * LAYERS,
        compiler_params=pltpu.CompilerParams(vmem_limit_bytes=12 * 1024 * 1024),
        cost_estimate=pl.CostEstimate(flops=flops, bytes_accessed=len(halves) * halves[0].size * 2, transcendentals=0),
        name="first",
    )(front, *base, *halves)


def assemble_kernel(count, *rest):
    blocks, outs = rest[:count], rest[count:]
    layers, cols, tile, _ = blocks[0].shape
    col = lax.axis_index("col")
    for layer in range(layers):
        for at, block in enumerate(blocks):
            side, flip, y = at // (2 * cols), at // 2 % cols, at % 2
            rows = pl.ds(pl.multiple_of((y * cols + (col ^ flip)) * tile, tile), tile)
            for t in range(cols):
                start = (side * cols + t) * tile
                outs[layer][rows, start : start + tile] = block[layer, t]


def assembled(near, far):
    layers, cols, tile, _ = near[0].shape
    span = 2 * cols * tile
    return pl.pallas_call(
        functools.partial(assemble_kernel, len(near + far)),
        out_shape=[jax.ShapeDtypeStruct((span, span), jnp.bfloat16)] * layers,
        in_specs=[IN_VMEM] * len(near + far),
        out_specs=[IN_VMEM] * layers,
        compiler_params=pltpu.CompilerParams(vmem_limit_bytes=20 * 1024 * 1024),
        cost_estimate=pl.CostEstimate(
            flops=0, bytes_accessed=4 * len(near + far) * near[0].size, transcendentals=0
        ),
        name="assemble",
    )(*near, *far)


def spread_kernel(found, keep, send):
    place = lax.axis_index("row") % 2 * lax.axis_size("col") + lax.axis_index("col")
    vert = keep.shape[-1]
    cols = lax.axis_size("col")
    for out, core in ((keep, 0), (send, 1)):
        for at in range(GROUP // 2):
            rel = 2 * at + core
            to = (rel & cols) | ((rel & (cols - 1)) ^ (place & (cols - 1)))
            out[at] = found[:, pl.ds(pl.multiple_of(to * vert, vert), vert)]


def spread_found(found):
    share, span = found.shape
    half = jax.ShapeDtypeStruct((GROUP // 2, share, span // GROUP), jnp.float32)
    return pl.pallas_call(
        spread_kernel,
        out_shape=[half] * 2,
        in_specs=[IN_VMEM],
        out_specs=[IN_VMEM] * 2,
        compiler_params=pltpu.CompilerParams(vmem_limit_bytes=4 * 1024 * 1024),
        name="spread",
    )(found)


def home_kernel(factor, *rest):
    pieces, out, words = rest[:-2], rest[-2], rest[-1]
    place = lax.axis_index("row") % 2 * lax.axis_size("col") + lax.axis_index("col")
    share = pieces[0].shape[-2]
    for at in range(2 * len(pieces)):
        rows = pl.multiple_of((place ^ at) * share, share)
        words[pl.ds(rows, share), :] = pieces[at // 2][at % 2]
    out[...] = words[...].T * factor[...]


def brought_home(factor, pieces):
    vert, sources = factor.shape
    return pl.pallas_call(
        home_kernel,
        out_shape=jax.ShapeDtypeStruct((vert, sources), jnp.float32),
        in_specs=[IN_VMEM] * (1 + len(pieces)),
        out_specs=IN_VMEM,
        scratch_shapes=[pltpu.VMEM((sources, vert), jnp.float32)],
        compiler_params=pltpu.CompilerParams(vmem_limit_bytes=4 * 1024 * 1024),
        name="home",
    )(factor, *pieces)


def traded(keep, send):
    got = swap(send, "col", 1)
    held = [jnp.stack([keep[at], got[at]]) for at in range(GROUP // 2)]
    from_y = swap(held[2], "row", 1)
    from_x = swap(held[1], "col", 2)
    from_d = lax.ppermute(held[3], ("row", "col"), diagonal())
    return [held[0], from_x, from_y, from_d]


def split_shards(paths_in, dep_in, levels, tile_src, pattern):
    vert, _ = paths_in.shape
    tile = pattern.shape[-1]

    own = packed_block(tile_src[0, 0].T, pattern[0, 0].reshape(-1, tile, tile))
    keep, send = packed_inputs(paths_in, dep_in, levels)
    pieces = traded(keep, send)
    by_y = [swap(own[1], "row", 1)]
    by_x = [swap(own[0], "col", 2)]
    by_core = [swap(half, "col", 1) for half in own]
    by_y.append(swap(own[0], "row", 1))
    by_x.append(swap(own[1], "col", 2))

    upper = jnp.where(levels == 0, paths_in, 1.0)[: vert // 2]
    lower = jnp.where(levels == 0, paths_in, 1.0)[vert // 2 :]
    upper, lower = lax.optimization_barrier((upper, lower))

    word, front = placed_inputs(pieces)
    masks = [word < 0.0, word == 0.5, word == 0.25, word >= 1.0]

    cross = [swap(by_y[0], "col", 2), swap(by_x[0], "row", 1)]
    crossed = [swap(by_x[0], "col", 1), swap(by_y[0], "col", 1)]
    crossed += [swap(by_x[1], "col", 1), swap(by_y[1], "col", 1)]
    near = list(own) + by_core + by_x + [crossed[0], crossed[2]]
    far = by_y + [crossed[1], crossed[3]]
    last = cross + [swap(half, "col", 1) for half in cross]
    first = first_terms(front, [], near + far)
    first = first_terms(front, first, last)
    whole = assembled(near, far + last)

    def forward(front, k):
        dims = (((1,), (1,)), ((), ()))
        return lax.dot_general(
            front.astype(jnp.bfloat16), whole[k], dims, preferred_element_type=jnp.float32
        )

    def across(value):
        return {k: swap(value(k), "row", 2 * k) for k in reversed(range(1, LAYERS))}

    counts = [None]
    for distance in (1, 2, 3):
        def terms(k):
            return first[k] if distance == 1 else forward(counts[-1], k)

        got = across(lambda k: coded(terms(k)))
        total = terms(0)
        for k in range(1, LAYERS):
            total = total + decoded(got[k])
        counts.append(jnp.where(masks[distance], total, 0.0))
    weight = (jnp.where(masks[3], word, 0.0) / jnp.maximum(counts[3], 1.0)).astype(jnp.bfloat16)
    found = jnp.zeros_like(word)
    for distance in (2, 1, 0):
        got = {0: weight} | across(lambda k: weight)
        back = sum(
            jnp.dot(got[k], whole[k], preferred_element_type=jnp.float32) for k in range(LAYERS)
        )
        if distance > 0:
            delta = counts[distance] * back
            found = found + delta
            weight = jnp.where(
                masks[distance], (1.0 + delta) / jnp.maximum(counts[distance], 1.0), 0.0
            ).astype(jnp.bfloat16)
        else:
            found = found + jnp.where(masks[0], back, 0.0)

    keep, send = spread_found(found)
    pieces = traded(keep, send)
    return brought_home(jnp.concatenate([upper, lower]), pieces)


def solution(mesh):
    placed = (
        P(("row", "col"), None),
        P(("row", "col"), None),
        P(("row", "col"), None),
        P("row", "col", None, None),
        P("row", "col", None, None, None, None),
    )

    def shards(paths_in, dep_in, levels, tile_src, pattern):
        rows, cols = lax.axis_size("row"), lax.axis_size("col")
        fits = (
            rows == 2 * LAYERS
            and 2 * cols == GROUP
            and paths_in.shape[0] == pattern.shape[-1]
            and tile_src.shape[3] == cols
            and paths_in.shape[1] % GROUP == 0
        )
        chosen = split_shards if fits else general_shards
        return chosen(paths_in, dep_in, levels, tile_src, pattern)

    return jax.shard_map(
        shards, mesh=mesh, in_specs=placed, out_specs=P(("row", "col"), None), check_vma=False
    )
```

```python
import functools

import jax
import jax.numpy as jnp
from jax import lax
from jax.experimental import pallas as pl
from jax.experimental.pallas import tpu as pltpu
from jax.sharding import PartitionSpec as P


def general_shards(paths_in, dep_in, levels, tile_src, pattern):
    vert_dev = paths_in.shape[0]
    tile_size = pattern.shape[-1]
    dest_tiles = tile_src.shape[2]
    band_slots = tile_src.shape[3]
    src_tiles = lax.axis_size("col") * vert_dev // tile_size
    per_source = dest_tiles * band_slots // src_tiles
    source_ids = tile_src[0, 0]
    tile_values = pattern[0, 0].astype(jnp.bfloat16)
    flat_ids = source_ids.reshape(-1)
    by_source = jnp.argsort(flat_ids, stable=True)
    back_values = tile_values.reshape(-1, tile_size, tile_size)[by_source]
    back_values = back_values.reshape(src_tiles, per_source, tile_size, tile_size)
    back_dest = (by_source // band_slots).reshape(src_tiles, per_source)

    def forward_terms(frontier):
        gathered = lax.all_gather(frontier, "col", axis=0, tiled=True)
        pieces = gathered.reshape(src_tiles, tile_size, gathered.shape[1])
        product = jnp.einsum(
            "ibrj,ibjs->irs", tile_values, pieces[source_ids], preferred_element_type=jnp.float32
        )
        terms = product.reshape(vert_dev * lax.axis_size("row"), product.shape[2])
        return lax.psum_scatter(terms, "row", scatter_dimension=0, tiled=True)

    def spread(weight):
        return lax.all_gather(weight, "row", axis=0, tiled=True)

    level_masks = [(levels == distance).astype(jnp.float32) for distance in range(4)]
    path_counts = [level_masks[0] * paths_in]
    for distance in (1, 2, 3):
        path_counts.append(
            level_masks[distance] * forward_terms(path_counts[-1].astype(jnp.bfloat16))
        )
    numerator = level_masks[3] * (1.0 + dep_in)
    spread_weight = spread((numerator / jnp.maximum(path_counts[3], 1.0)).astype(jnp.bfloat16))
    dependency = jnp.zeros(paths_in.shape, jnp.float32)
    for distance in (2, 1, 0):
        backward_pieces = spread_weight.reshape(dest_tiles, tile_size, spread_weight.shape[1])
        source_product = jnp.einsum(
            "tgrj,tgrs->tjs",
            back_values,
            backward_pieces[back_dest],
            preferred_element_type=jnp.float32,
        )
        source_product = source_product.reshape(
            vert_dev * lax.axis_size("col"), source_product.shape[2]
        )
        dependence = (
            level_masks[distance]
            * path_counts[distance]
            * lax.psum_scatter(source_product, "col", scatter_dimension=0, tiled=True)
        )
        dependency = dependency + dependence
        if distance > 0:
            weight = (
                level_masks[distance] * (1.0 + dependence) / jnp.maximum(path_counts[distance], 1.0)
            ).astype(jnp.bfloat16)
            spread_weight = spread(weight)
    return dependency


def partner(axis, bit):
    return [(i, i ^ bit) for i in range(lax.axis_size(axis))]


def swap(value, axis, bit):
    return lax.ppermute(value, axis, partner(axis, bit))


def diagonal():
    cols = lax.axis_size("col")
    return [(i, i ^ cols ^ 2) for i in range(lax.axis_size("row") * cols)]


GROUP = 8
LAYERS = 4
LOWEST = 5
MANTISSA = 18
BYTE = 255


def coded(count):
    scaled = count * 2.0**LOWEST
    exponent = jnp.zeros_like(count)
    for bit in (32, 16, 8, 4, 2, 1):
        large = scaled >= 2.0**bit
        scaled = jnp.where(large, scaled * 2.0**-bit, scaled)
        exponent = exponent + jnp.where(large, float(bit), 0.0)
    mantissa = jnp.floor((scaled - 1.0) * 2.0**MANTISSA + 0.5)
    code = jnp.where(count > 0.0, exponent * 2.0**MANTISSA + mantissa, 0.0).astype(jnp.int32)
    *first, last = jnp.split(code, 4, axis=1)
    words = [part | (((last >> (8 * at)) & BYTE) << 24) for at, part in enumerate(first)]
    return jnp.concatenate(words, axis=1)


def decoded(words):
    words = jnp.split(words, 3, axis=1)
    last = sum(((word >> 24) & BYTE) << (8 * at) for at, word in enumerate(words))
    code = jnp.concatenate([word & (2**24 - 1) for word in words] + [last], axis=1)
    exponent = code >> MANTISSA
    mantissa = code & (2**MANTISSA - 1)
    count = mantissa.astype(jnp.float32) * 2.0 ** (-MANTISSA - LOWEST) + 2.0**-LOWEST
    for bit in (32, 16, 8, 4, 2, 1):
        count = jnp.where((exponent & bit) != 0, count * 2.0**bit, count)
    return jnp.where(code > 0, count, 0.0)


IN_VMEM = pl.BlockSpec(memory_space=pltpu.VMEM)
IN_SMEM = pl.BlockSpec(memory_space=pltpu.SMEM)


def pack_kernel(ids, pattern, *outs):
    cols = outs[0].shape[1]
    row = lax.axis_index("row")
    for layer in reversed(range(LAYERS)):
        for y in range(2):
            i = row ^ (2 * layer + y)
            for t in range(cols):
                slot = jnp.int32(0)
                for e in range(1, cols):
                    slot = jnp.where(ids[e, i] == t, e, slot)
                tile = pattern[i * cols + slot].astype(jnp.float32).astype(jnp.bfloat16)
                if layer:
                    outs[y][layer - 1, t] = tile
                else:
                    outs[2][y, t] = tile
                    outs[3][1 - y, t] = tile


def packed_block(ids, pattern):
    cols, tile = ids.shape[0], pattern.shape[-1]
    other = jax.ShapeDtypeStruct((LAYERS - 1, cols, tile, tile), jnp.bfloat16)
    own = jax.ShapeDtypeStruct((2, cols, tile, tile), jnp.bfloat16)
    return pl.pallas_call(
        pack_kernel,
        out_shape=[other, other, own, own],
        in_specs=[IN_SMEM, IN_VMEM],
        out_specs=[IN_VMEM] * 4,
        compiler_params=pltpu.CompilerParams(vmem_limit_bytes=8 * 1024 * 1024),
        name="pack",
    )(ids, pattern)


def inputs_kernel(paths_in, dep_in, levels, keep, send, words):
    level = levels[...]
    word = jnp.where(
        level == 0, -paths_in[...], jnp.where(level == 3, 1.0 + dep_in[...], 0.0)
    )
    word = jnp.where(level == 1, 0.5, jnp.where(level == 2, 0.25, word))
    words[...] = word.T
    share = keep.shape[-2]
    place = lax.axis_index("row") % 2 * lax.axis_size("col") + lax.axis_index("col")
    for out, core in ((keep, 0), (send, 1)):
        for at in range(GROUP // 2):
            rows = pl.multiple_of((place ^ (2 * at + core)) * share, share)
            out[at] = words[pl.ds(rows, share), :]


def packed_inputs(paths_in, dep_in, levels):
    vert, sources = paths_in.shape
    half = jax.ShapeDtypeStruct((GROUP // 2, sources // GROUP, vert), jnp.float32)
    return pl.pallas_call(
        inputs_kernel,
        out_shape=[half] * 2,
        in_specs=[IN_VMEM] * 3,
        out_specs=[IN_VMEM] * 2,
        scratch_shapes=[pltpu.VMEM((sources, vert), jnp.float32)],
        compiler_params=pltpu.CompilerParams(vmem_limit_bytes=4 * 1024 * 1024),
        name="inputs",
    )(paths_in, dep_in, levels)


def placed_kernel(*rest):
    pieces, word, front = rest[:-2], rest[-2], rest[-1]
    vert = pieces[0].shape[-1]
    col = lax.axis_index("col")
    for at in range(2 * len(pieces)):
        to = (at & 4) | ((at & 3) ^ col)
        piece = pieces[at // 2][at % 2]
        lanes = pl.ds(pl.multiple_of(to * vert, vert), vert)
        word[:, lanes] = piece
        front[:, lanes] = jnp.maximum(-piece, 0.0).astype(jnp.bfloat16)


def placed_inputs(pieces):
    _, share, vert = pieces[0].shape
    shape = (share, 2 * len(pieces) * vert)
    return pl.pallas_call(
        placed_kernel,
        out_shape=[jax.ShapeDtypeStruct(shape, kind) for kind in (jnp.float32, jnp.bfloat16)],
        in_specs=[IN_VMEM] * len(pieces),
        out_specs=[IN_VMEM] * 2,
        compiler_params=pltpu.CompilerParams(vmem_limit_bytes=4 * 1024 * 1024),
        name="placed",
    )(*pieces)


def rows_of(halves, layer):
    cols = halves[0].shape[1]
    return jnp.concatenate(
        [jnp.concatenate([half[layer, t] for t in range(cols)], axis=1) for half in halves], axis=0
    )


def first_kernel(base, front, *rest):
    count = LAYERS - 1
    outs = rest[-count:]
    start = rest[:count] if base else None
    halves = rest[count if base else 0 : -count]
    pairs = ((1, 2), (1, 3)) if base else tuple((at // 4, at % 4) for at in range(6))
    layers, cols, tile, _ = halves[0].shape
    wide = cols * tile
    col = lax.axis_index("col")
    for layer in reversed(range(layers)):
        for flip in range(cols):
            terms = None
            for at, (side, c) in enumerate(pairs):
                if c == flip:
                    term = lax.dot_general(
                        front[:, side * wide : (side + 1) * wide],
                        rows_of(halves[2 * at : 2 * at + 2], layer),
                        (((1,), (1,)), ((), ())),
                        preferred_element_type=jnp.float32,
                    )
                    terms = term if terms is None else terms + term
            for y in range(2):
                lanes = pl.ds(pl.multiple_of((y * cols + (col ^ flip)) * tile, tile), tile)
                if terms is None:
                    outs[layer][:, lanes] = start[layer][:, lanes]
                    continue
                part = terms[:, y * tile : (y + 1) * tile]
                outs[layer][:, lanes] = part + start[layer][:, lanes] if base else part


def first_terms(front, base, halves):
    shape = jax.ShapeDtypeStruct(front.shape, jnp.float32)
    count = LAYERS - 1
    size = len(halves) * halves[0].size
    return pl.pallas_call(
        functools.partial(first_kernel, bool(base)),
        out_shape=[shape] * count,
        in_specs=[IN_VMEM] * (1 + len(base) + len(halves)),
        out_specs=[IN_VMEM] * count,
        compiler_params=pltpu.CompilerParams(vmem_limit_bytes=12 * 1024 * 1024),
        cost_estimate=pl.CostEstimate(
            flops=2 * front.shape[0] * size, bytes_accessed=2 * size, transcendentals=0
        ),
        name="first",
    )(front, *base, *halves)


def assemble_kernel(parts, count, *rest):
    blocks, outs = rest[:count], rest[count:]
    _, cols, tile, _ = blocks[0].shape
    col = lax.axis_index("col")
    for layer, out in enumerate(outs):
        for at in range(count * 2 // parts):
            side, flip, y = at // (2 * cols), at // 2 % cols, at % 2
            block, lead = (blocks[at], layer) if parts == 2 else (blocks[at // 2], y)
            rows = pl.ds(pl.multiple_of((y * cols + (col ^ flip)) * tile, tile), tile)
            for t in range(cols):
                start = (side * cols + t) * tile
                out[rows, start : start + tile] = block[lead, t]


def assembled(blocks, parts):
    lead, cols, tile, _ = blocks[0].shape
    span = 2 * cols * tile
    layers = lead if parts == 2 else 1
    return pl.pallas_call(
        functools.partial(assemble_kernel, parts, len(blocks)),
        out_shape=[jax.ShapeDtypeStruct((span, span), jnp.bfloat16)] * layers,
        in_specs=[IN_VMEM] * len(blocks),
        out_specs=[IN_VMEM] * layers,
        compiler_params=pltpu.CompilerParams(vmem_limit_bytes=16 * 1024 * 1024),
        cost_estimate=pl.CostEstimate(
            flops=0, bytes_accessed=4 * len(blocks) * blocks[0].size, transcendentals=0
        ),
        name="assemble",
    )(*blocks)


def spread_kernel(found, keep, send):
    place = lax.axis_index("row") % 2 * lax.axis_size("col") + lax.axis_index("col")
    vert = keep.shape[-1]
    cols = lax.axis_size("col")
    for out, core in ((keep, 0), (send, 1)):
        for at in range(GROUP // 2):
            rel = 2 * at + core
            to = (rel & cols) | ((rel & (cols - 1)) ^ (place & (cols - 1)))
            out[at] = found[:, pl.ds(pl.multiple_of(to * vert, vert), vert)]


def spread_found(found):
    share, span = found.shape
    half = jax.ShapeDtypeStruct((GROUP // 2, share, span // GROUP), jnp.float32)
    return pl.pallas_call(
        spread_kernel,
        out_shape=[half] * 2,
        in_specs=[IN_VMEM],
        out_specs=[IN_VMEM] * 2,
        compiler_params=pltpu.CompilerParams(vmem_limit_bytes=4 * 1024 * 1024),
        name="spread",
    )(found)


def home_kernel(factor, *rest):
    pieces, out, words = rest[:-2], rest[-2], rest[-1]
    place = lax.axis_index("row") % 2 * lax.axis_size("col") + lax.axis_index("col")
    share = pieces[0].shape[-2]
    for at in range(2 * len(pieces)):
        rows = pl.multiple_of((place ^ at) * share, share)
        words[pl.ds(rows, share), :] = pieces[at // 2][at % 2]
    out[...] = words[...].T * factor[...]


def brought_home(factor, pieces):
    vert, sources = factor.shape
    return pl.pallas_call(
        home_kernel,
        out_shape=jax.ShapeDtypeStruct((vert, sources), jnp.float32),
        in_specs=[IN_VMEM] * (1 + len(pieces)),
        out_specs=IN_VMEM,
        scratch_shapes=[pltpu.VMEM((sources, vert), jnp.float32)],
        compiler_params=pltpu.CompilerParams(vmem_limit_bytes=4 * 1024 * 1024),
        name="home",
    )(factor, *pieces)


def traded(keep, send):
    got = swap(send, "col", 1)
    held = [jnp.stack([keep[at], got[at]]) for at in range(GROUP // 2)]
    from_y = swap(held[2], "row", 1)
    from_x = swap(held[1], "col", 2)
    from_d = lax.ppermute(held[3], ("row", "col"), diagonal())
    return [held[0], from_x, from_y, from_d]


def split_shards(paths_in, dep_in, levels, tile_src, pattern):
    vert, _ = paths_in.shape
    tile = pattern.shape[-1]

    *own, same, flipped = packed_block(tile_src[0, 0].T, pattern[0, 0].reshape(-1, tile, tile))
    keep, send = packed_inputs(paths_in, dep_in, levels)
    pieces = traded(keep, send)
    by_y = [swap(own[1], "row", 1)]
    by_x = [swap(own[0], "col", 2)]
    by_core = [swap(half, "col", 1) for half in own]
    by_y.append(swap(own[0], "row", 1))
    by_x.append(swap(own[1], "col", 2))

    upper = jnp.where(levels == 0, paths_in, 1.0)[: vert // 2]
    lower = jnp.where(levels == 0, paths_in, 1.0)[vert // 2 :]
    upper, lower = lax.optimization_barrier((upper, lower))

    word, front = placed_inputs(pieces)
    masks = [word < 0.0, word == 0.5, word == 0.25, word >= 1.0]

    cross = [swap(by_y[0], "col", 2), swap(by_x[0], "row", 1)]
    same_y = swap(flipped, "row", 1)
    same_x = swap(same, "col", 2)
    same_d = lax.ppermute(flipped, ("row", "col"), diagonal())
    crossed = [swap(by_x[0], "col", 1), swap(by_y[0], "col", 1)]
    crossed += [swap(by_x[1], "col", 1), swap(by_y[1], "col", 1)]
    near = list(own) + by_core + by_x + [crossed[0], crossed[2]]
    far = by_y + [crossed[1], crossed[3]]
    last = cross + [swap(half, "col", 1) for half in cross]
    first = first_terms(front, [], near + far)
    first = first_terms(front, first, last)
    blocks = [
        part
        for block in (same, same_x, same_y, same_d)
        for part in (block, swap(block, "col", 1))
    ]
    whole = assembled(blocks, 1) + assembled(near + far + last, 2)

    def forward(front, k):
        dims = (((1,), (1,)), ((), ()))
        return lax.dot_general(
            front.astype(jnp.bfloat16), whole[k], dims, preferred_element_type=jnp.float32
        )

    def across(value):
        return {k: swap(value(k), "row", 2 * k) for k in reversed(range(1, LAYERS))}

    counts = [None]
    for distance in (1, 2, 3):
        def terms(k):
            return forward(counts[-1], k) if distance > 1 else first[k - 1]

        got = across(lambda k: coded(terms(k)))
        total = forward(front if distance == 1 else counts[-1], 0)
        for k in range(1, LAYERS):
            total = total + decoded(got[k])
        counts.append(jnp.where(masks[distance], total, 0.0))
    weight = (jnp.where(masks[3], word, 0.0) / jnp.maximum(counts[3], 1.0)).astype(jnp.bfloat16)
    found = jnp.zeros_like(word)
    for distance in (2, 1, 0):
        got = {0: weight} | across(lambda k: weight)
        back = sum(
            jnp.dot(got[k], whole[k], preferred_element_type=jnp.float32) for k in range(LAYERS)
        )
        if distance > 0:
            delta = counts[distance] * back
            found = found + delta
            weight = jnp.where(
                masks[distance], (1.0 + delta) / jnp.maximum(counts[distance], 1.0), 0.0
            ).astype(jnp.bfloat16)
        else:
            found = found + jnp.where(masks[0], back, 0.0)

    keep, send = spread_found(found)
    pieces = traded(keep, send)
    return brought_home(jnp.concatenate([upper, lower]), pieces)


def solution(mesh):
    placed = (
        P(("row", "col"), None),
        P(("row", "col"), None),
        P(("row", "col"), None),
        P("row", "col", None, None),
        P("row", "col", None, None, None, None),
    )

    def shards(paths_in, dep_in, levels, tile_src, pattern):
        rows, cols = lax.axis_size("row"), lax.axis_size("col")
        fits = (
            rows == 2 * LAYERS
            and 2 * cols == GROUP
            and paths_in.shape[0] == pattern.shape[-1]
            and tile_src.shape[3] == cols
            and paths_in.shape[1] % GROUP == 0
        )
        chosen = split_shards if fits else general_shards
        return chosen(paths_in, dep_in, levels, tile_src, pattern)

    return jax.shard_map(
        shards, mesh=mesh, in_specs=placed, out_specs=P(("row", "col"), None), check_vma=False
    )
```

```python
import functools

import jax
import jax.numpy as jnp
from jax import lax
from jax.experimental import pallas as pl
from jax.experimental.pallas import tpu as pltpu
from jax.sharding import PartitionSpec as P


def general_shards(paths_in, dep_in, levels, tile_src, pattern):
    vert_dev = paths_in.shape[0]
    tile_size = pattern.shape[-1]
    dest_tiles = tile_src.shape[2]
    band_slots = tile_src.shape[3]
    src_tiles = lax.axis_size("col") * vert_dev // tile_size
    per_source = dest_tiles * band_slots // src_tiles
    source_ids = tile_src[0, 0]
    tile_values = pattern[0, 0].astype(jnp.bfloat16)
    flat_ids = source_ids.reshape(-1)
    by_source = jnp.argsort(flat_ids, stable=True)
    back_values = tile_values.reshape(-1, tile_size, tile_size)[by_source]
    back_values = back_values.reshape(src_tiles, per_source, tile_size, tile_size)
    back_dest = (by_source // band_slots).reshape(src_tiles, per_source)

    def forward_terms(frontier):
        gathered = lax.all_gather(frontier, "col", axis=0, tiled=True)
        pieces = gathered.reshape(src_tiles, tile_size, gathered.shape[1])
        product = jnp.einsum(
            "ibrj,ibjs->irs", tile_values, pieces[source_ids], preferred_element_type=jnp.float32
        )
        terms = product.reshape(vert_dev * lax.axis_size("row"), product.shape[2])
        return lax.psum_scatter(terms, "row", scatter_dimension=0, tiled=True)

    def spread(weight):
        return lax.all_gather(weight, "row", axis=0, tiled=True)

    level_masks = [(levels == distance).astype(jnp.float32) for distance in range(4)]
    path_counts = [level_masks[0] * paths_in]
    for distance in (1, 2, 3):
        path_counts.append(
            level_masks[distance] * forward_terms(path_counts[-1].astype(jnp.bfloat16))
        )
    numerator = level_masks[3] * (1.0 + dep_in)
    spread_weight = spread((numerator / jnp.maximum(path_counts[3], 1.0)).astype(jnp.bfloat16))
    dependency = jnp.zeros(paths_in.shape, jnp.float32)
    for distance in (2, 1, 0):
        backward_pieces = spread_weight.reshape(dest_tiles, tile_size, spread_weight.shape[1])
        source_product = jnp.einsum(
            "tgrj,tgrs->tjs",
            back_values,
            backward_pieces[back_dest],
            preferred_element_type=jnp.float32,
        )
        source_product = source_product.reshape(
            vert_dev * lax.axis_size("col"), source_product.shape[2]
        )
        dependence = (
            level_masks[distance]
            * path_counts[distance]
            * lax.psum_scatter(source_product, "col", scatter_dimension=0, tiled=True)
        )
        dependency = dependency + dependence
        if distance > 0:
            weight = (
                level_masks[distance] * (1.0 + dependence) / jnp.maximum(path_counts[distance], 1.0)
            ).astype(jnp.bfloat16)
            spread_weight = spread(weight)
    return dependency


def partner(axis, bit):
    return [(i, i ^ bit) for i in range(lax.axis_size(axis))]


def swap(value, axis, bit):
    return lax.ppermute(value, axis, partner(axis, bit))


def diagonal():
    cols = lax.axis_size("col")
    return [(i, i ^ cols ^ 2) for i in range(lax.axis_size("row") * cols)]


GROUP = 8
LAYERS = 4
LOWEST = 5
MANTISSA = 18
BYTE = 255


def coded(count):
    scaled = count * 2.0**LOWEST
    exponent = jnp.zeros_like(count)
    for bit in (32, 16, 8, 4, 2, 1):
        large = scaled >= 2.0**bit
        scaled = jnp.where(large, scaled * 2.0**-bit, scaled)
        exponent = exponent + jnp.where(large, float(bit), 0.0)
    mantissa = jnp.floor((scaled - 1.0) * 2.0**MANTISSA + 0.5)
    code = jnp.where(count > 0.0, exponent * 2.0**MANTISSA + mantissa, 0.0).astype(jnp.int32)
    *first, last = jnp.split(code, 4, axis=1)
    words = [part | (((last >> (8 * at)) & BYTE) << 24) for at, part in enumerate(first)]
    return jnp.concatenate(words, axis=1)


def decoded(words):
    words = jnp.split(words, 3, axis=1)
    last = sum(((word >> 24) & BYTE) << (8 * at) for at, word in enumerate(words))
    code = jnp.concatenate([word & (2**24 - 1) for word in words] + [last], axis=1)
    exponent = code >> MANTISSA
    mantissa = code & (2**MANTISSA - 1)
    count = mantissa.astype(jnp.float32) * 2.0 ** (-MANTISSA - LOWEST) + 2.0**-LOWEST
    for bit in (32, 16, 8, 4, 2, 1):
        count = jnp.where((exponent & bit) != 0, count * 2.0**bit, count)
    return jnp.where(code > 0, count, 0.0)


IN_VMEM = pl.BlockSpec(memory_space=pltpu.VMEM)
IN_SMEM = pl.BlockSpec(memory_space=pltpu.SMEM)


def pack_kernel(ids, pattern, *outs):
    cols = outs[0].shape[1]
    row = lax.axis_index("row")
    for layer in reversed(range(LAYERS)):
        for y in range(2):
            i = row ^ (2 * layer + y)
            for t in range(cols):
                slot = jnp.int32(0)
                for e in range(1, cols):
                    slot = jnp.where(ids[e, i] == t, e, slot)
                tile = pattern[i * cols + slot].astype(jnp.float32).astype(jnp.bfloat16)
                if layer:
                    outs[y][layer - 1, t] = tile
                else:
                    outs[2][y, t] = tile
                    outs[3][1 - y, t] = tile


def packed_block(ids, pattern):
    cols, tile = ids.shape[0], pattern.shape[-1]
    other = jax.ShapeDtypeStruct((LAYERS - 1, cols, tile, tile), jnp.bfloat16)
    own = jax.ShapeDtypeStruct((2, cols, tile, tile), jnp.bfloat16)
    return pl.pallas_call(
        pack_kernel,
        out_shape=[other, other, own, own],
        in_specs=[IN_SMEM, IN_VMEM],
        out_specs=[IN_VMEM] * 4,
        compiler_params=pltpu.CompilerParams(vmem_limit_bytes=8 * 1024 * 1024),
        name="pack",
    )(ids, pattern)


def inputs_kernel(paths_in, dep_in, levels, keep, send, words):
    level = levels[...]
    word = jnp.where(
        level == 0, -paths_in[...], jnp.where(level == 3, 1.0 + dep_in[...], 0.0)
    )
    word = jnp.where(level == 1, 0.5, jnp.where(level == 2, 0.25, word))
    words[...] = word.T
    share = keep.shape[-2]
    place = lax.axis_index("row") % 2 * lax.axis_size("col") + lax.axis_index("col")
    for out, core in ((keep, 0), (send, 1)):
        for at in range(GROUP // 2):
            rows = pl.multiple_of((place ^ (2 * at + core)) * share, share)
            out[at] = words[pl.ds(rows, share), :]


def packed_inputs(paths_in, dep_in, levels):
    vert, sources = paths_in.shape
    half = jax.ShapeDtypeStruct((GROUP // 2, sources // GROUP, vert), jnp.float32)
    return pl.pallas_call(
        inputs_kernel,
        out_shape=[half] * 2,
        in_specs=[IN_VMEM] * 3,
        out_specs=[IN_VMEM] * 2,
        scratch_shapes=[pltpu.VMEM((sources, vert), jnp.float32)],
        compiler_params=pltpu.CompilerParams(vmem_limit_bytes=4 * 1024 * 1024),
        name="inputs",
    )(paths_in, dep_in, levels)


def placed_kernel(*rest):
    pieces, word, front = rest[:-2], rest[-2], rest[-1]
    vert = pieces[0].shape[-1]
    col = lax.axis_index("col")
    for at in range(2 * len(pieces)):
        to = (at & 4) | ((at & 3) ^ col)
        piece = pieces[at // 2][at % 2]
        lanes = pl.ds(pl.multiple_of(to * vert, vert), vert)
        word[:, lanes] = piece
        front[:, lanes] = jnp.maximum(-piece, 0.0).astype(jnp.bfloat16)


def placed_inputs(pieces):
    _, share, vert = pieces[0].shape
    shape = (share, 2 * len(pieces) * vert)
    return pl.pallas_call(
        placed_kernel,
        out_shape=[jax.ShapeDtypeStruct(shape, kind) for kind in (jnp.float32, jnp.bfloat16)],
        in_specs=[IN_VMEM] * len(pieces),
        out_specs=[IN_VMEM] * 2,
        compiler_params=pltpu.CompilerParams(vmem_limit_bytes=4 * 1024 * 1024),
        name="placed",
    )(*pieces)


def rows_of(halves, layer):
    cols = halves[0].shape[1]
    return jnp.concatenate(
        [jnp.concatenate([half[layer, t] for t in range(cols)], axis=1) for half in halves], axis=0
    )


def first_kernel(base, front, *rest):
    count = LAYERS - 1
    outs = rest[-count:]
    start = rest[:count] if base else None
    halves = rest[count if base else 0 : -count]
    pairs = ((1, 2), (1, 3)) if base else tuple((at // 4, at % 4) for at in range(6))
    layers, cols, tile, _ = halves[0].shape
    wide = cols * tile
    col = lax.axis_index("col")
    for layer in reversed(range(layers)):
        for flip in range(cols):
            terms = None
            for at, (side, c) in enumerate(pairs):
                if c == flip:
                    term = lax.dot_general(
                        front[:, side * wide : (side + 1) * wide],
                        rows_of(halves[2 * at : 2 * at + 2], layer),
                        (((1,), (1,)), ((), ())),
                        preferred_element_type=jnp.float32,
                    )
                    terms = term if terms is None else terms + term
            for y in range(2):
                lanes = pl.ds(pl.multiple_of((y * cols + (col ^ flip)) * tile, tile), tile)
                if terms is None:
                    outs[layer][:, lanes] = start[layer][:, lanes]
                    continue
                part = terms[:, y * tile : (y + 1) * tile]
                outs[layer][:, lanes] = part + start[layer][:, lanes] if base else part


def first_terms(front, base, halves):
    shape = jax.ShapeDtypeStruct(front.shape, jnp.float32)
    count = LAYERS - 1
    size = len(halves) * halves[0].size
    return pl.pallas_call(
        functools.partial(first_kernel, bool(base)),
        out_shape=[shape] * count,
        in_specs=[IN_VMEM] * (1 + len(base) + len(halves)),
        out_specs=[IN_VMEM] * count,
        compiler_params=pltpu.CompilerParams(vmem_limit_bytes=12 * 1024 * 1024),
        cost_estimate=pl.CostEstimate(
            flops=2 * front.shape[0] * size, bytes_accessed=2 * size, transcendentals=0
        ),
        name="first",
    )(front, *base, *halves)


def assemble_kernel(parts, count, *rest):
    blocks, outs = rest[:count], rest[count:]
    _, cols, tile, _ = blocks[0].shape
    col = lax.axis_index("col")
    for layer, out in enumerate(outs):
        for at in range(count * 2 // parts):
            side, flip, y = at // (2 * cols), at // 2 % cols, at % 2
            block, lead = (blocks[at], layer) if parts == 2 else (blocks[at // 2], y)
            rows = pl.ds(pl.multiple_of((y * cols + (col ^ flip)) * tile, tile), tile)
            for t in range(cols):
                start = (side * cols + t) * tile
                out[rows, start : start + tile] = block[lead, t]


def assembled(blocks, parts):
    lead, cols, tile, _ = blocks[0].shape
    span = 2 * cols * tile
    layers = lead if parts == 2 else 1
    return pl.pallas_call(
        functools.partial(assemble_kernel, parts, len(blocks)),
        out_shape=[jax.ShapeDtypeStruct((span, span), jnp.bfloat16)] * layers,
        in_specs=[IN_VMEM] * len(blocks),
        out_specs=[IN_VMEM] * layers,
        compiler_params=pltpu.CompilerParams(vmem_limit_bytes=16 * 1024 * 1024),
        cost_estimate=pl.CostEstimate(
            flops=0, bytes_accessed=4 * len(blocks) * blocks[0].size, transcendentals=0
        ),
        name="assemble",
    )(*blocks)


def lead_kernel(mask, own, *rest):
    got, word, whole, count, front, words = rest[:-5], rest[-5], rest[-4], rest[-3], rest[-2], rest[-1]
    total = own[...]
    for message in got:
        total = total + decoded(message[...])
    total = jnp.where(mask(word[...]), total, 0.0)
    count[...] = total
    front[...] = total.astype(jnp.bfloat16)
    words[...] = coded(across_terms(front[...], whole[...]))


def across_terms(front, whole):
    return lax.dot_general(
        front, whole, (((1,), (1,)), ((), ())), preferred_element_type=jnp.float32
    )


def message_kernel(front, whole, words):
    words[...] = coded(across_terms(front[...], whole[...]))


def vmem_call(kernel, outs, args, flops):
    moved = sum(x.size * x.dtype.itemsize for x in (*outs, *args))
    return pl.pallas_call(
        kernel,
        out_shape=outs,
        in_specs=[IN_VMEM] * len(args),
        out_specs=[IN_VMEM] * len(outs),
        compiler_params=pltpu.CompilerParams(vmem_limit_bytes=8 * 1024 * 1024),
        cost_estimate=pl.CostEstimate(flops=flops, bytes_accessed=moved, transcendentals=0),
    )(*args)


def level_terms(mask, own, got, word, whole):
    share, span = own.shape
    outs = [
        jax.ShapeDtypeStruct((share, span), jnp.float32),
        jax.ShapeDtypeStruct((share, span), jnp.bfloat16),
        jax.ShapeDtypeStruct((share, span // 4 * 3), jnp.int32),
    ]
    flops = 2 * share * whole.size
    return vmem_call(functools.partial(lead_kernel, mask), outs, [own, *got, word, whole], flops)


def message(front, whole):
    share, span = front.shape
    outs = [jax.ShapeDtypeStruct((share, span // 4 * 3), jnp.int32)]
    return vmem_call(message_kernel, outs, [front, whole], 2 * share * whole.size)[0]


def back_kernel(mask, last, part, weight, whole, *rest):
    out = rest[-1]
    back = part[...] + jnp.dot(weight[...], whole[...], preferred_element_type=jnp.float32)
    if last:
        found, word = rest[0], rest[1]
        out[...] = found[...] + jnp.where(mask(word[...]), back, 0.0)
        return
    count, found, word, grown = rest[0], rest[1], rest[2], rest[3]
    delta = count[...] * back
    grown[...] = found[...] + delta
    new = jnp.where(mask(word[...]), (1.0 + delta) / jnp.maximum(count[...], 1.0), 0.0)
    out[...] = new.astype(jnp.bfloat16)


def back_terms(mask, part, weight, whole, count, found, word):
    last = count is None
    outs = [jax.ShapeDtypeStruct(found.shape, jnp.float32)]
    if not last:
        outs.append(jax.ShapeDtypeStruct(found.shape, jnp.bfloat16))
    args = [part, weight, whole] + ([] if last else [count]) + [found, word]
    flops = 2 * found.shape[0] * whole.size
    return vmem_call(functools.partial(back_kernel, mask, last), outs, args, flops)


MASKS = (
    lambda word: word < 0.0,
    lambda word: word == 0.5,
    lambda word: word == 0.25,
    lambda word: word >= 1.0,
)


def spread_kernel(found, keep, send):
    place = lax.axis_index("row") % 2 * lax.axis_size("col") + lax.axis_index("col")
    vert = keep.shape[-1]
    cols = lax.axis_size("col")
    for out, core in ((keep, 0), (send, 1)):
        for at in range(GROUP // 2):
            rel = 2 * at + core
            to = (rel & cols) | ((rel & (cols - 1)) ^ (place & (cols - 1)))
            out[at] = found[:, pl.ds(pl.multiple_of(to * vert, vert), vert)]


def spread_found(found):
    share, span = found.shape
    half = jax.ShapeDtypeStruct((GROUP // 2, share, span // GROUP), jnp.float32)
    return pl.pallas_call(
        spread_kernel,
        out_shape=[half] * 2,
        in_specs=[IN_VMEM],
        out_specs=[IN_VMEM] * 2,
        compiler_params=pltpu.CompilerParams(vmem_limit_bytes=4 * 1024 * 1024),
        name="spread",
    )(found)


def home_kernel(factor, *rest):
    pieces, out, words = rest[:-2], rest[-2], rest[-1]
    place = lax.axis_index("row") % 2 * lax.axis_size("col") + lax.axis_index("col")
    share = pieces[0].shape[-2]
    for at in range(2 * len(pieces)):
        rows = pl.multiple_of((place ^ at) * share, share)
        words[pl.ds(rows, share), :] = pieces[at // 2][at % 2]
    out[...] = words[...].T * factor[...]


def brought_home(factor, pieces):
    vert, sources = factor.shape
    return pl.pallas_call(
        home_kernel,
        out_shape=jax.ShapeDtypeStruct((vert, sources), jnp.float32),
        in_specs=[IN_VMEM] * (1 + len(pieces)),
        out_specs=IN_VMEM,
        scratch_shapes=[pltpu.VMEM((sources, vert), jnp.float32)],
        compiler_params=pltpu.CompilerParams(vmem_limit_bytes=4 * 1024 * 1024),
        name="home",
    )(factor, *pieces)


def traded(keep, send):
    got = swap(send, "col", 1)
    held = [jnp.stack([keep[at], got[at]]) for at in range(GROUP // 2)]
    from_y = swap(held[2], "row", 1)
    from_x = swap(held[1], "col", 2)
    from_d = lax.ppermute(held[3], ("row", "col"), diagonal())
    return [held[0], from_x, from_y, from_d]


def split_shards(paths_in, dep_in, levels, tile_src, pattern):
    vert, _ = paths_in.shape
    tile = pattern.shape[-1]

    *own, same, flipped = packed_block(tile_src[0, 0].T, pattern[0, 0].reshape(-1, tile, tile))
    keep, send = packed_inputs(paths_in, dep_in, levels)
    pieces = traded(keep, send)
    by_y = [swap(own[1], "row", 1)]
    by_x = [swap(own[0], "col", 2)]
    by_core = [swap(half, "col", 1) for half in own]
    by_y.append(swap(own[0], "row", 1))
    by_x.append(swap(own[1], "col", 2))

    upper = jnp.where(levels == 0, paths_in, 1.0)[: vert // 2]
    lower = jnp.where(levels == 0, paths_in, 1.0)[vert // 2 :]
    upper, lower = lax.optimization_barrier((upper, lower))

    word, front = placed_inputs(pieces)
    cross = [swap(by_y[0], "col", 2), swap(by_x[0], "row", 1)]
    same_y = swap(flipped, "row", 1)
    same_x = swap(same, "col", 2)
    same_d = lax.ppermute(flipped, ("row", "col"), diagonal())
    crossed = [swap(by_x[0], "col", 1), swap(by_y[0], "col", 1)]
    crossed += [swap(by_x[1], "col", 1), swap(by_y[1], "col", 1)]
    near = list(own) + by_core + by_x + [crossed[0], crossed[2]]
    far = by_y + [crossed[1], crossed[3]]
    last = cross + [swap(half, "col", 1) for half in cross]
    first = first_terms(front, [], near + far)
    first = first_terms(front, first, last)
    blocks = [
        part
        for block in (same, same_x, same_y, same_d)
        for part in (block, swap(block, "col", 1))
    ]
    whole = assembled(blocks, 1) + assembled(near + far + last, 2)

    def across(value):
        got = {}
        for k in reversed(range(1, LAYERS)):
            got[k] = swap(value(k), "row", 2 * k)
        return got

    got = across(lambda k: coded(first[k - 1]))
    counts = []
    for distance in (1, 2):
        own = across_terms(front, whole[0])
        got = [got[k] for k in range(1, LAYERS)]
        count, front, words = level_terms(MASKS[distance], own, got, word, whole[-1])
        counts.append(count)
        got = across(lambda k: words if k == LAYERS - 1 else message(front, whole[k]))
    total = across_terms(front, whole[0])
    for k in range(1, LAYERS):
        total = total + decoded(got[k])
    weight = jnp.where(MASKS[3](word), word / jnp.maximum(total, 1.0), 0.0).astype(jnp.bfloat16)
    found = jnp.zeros_like(word)
    for distance in (2, 1, 0):
        got = across(lambda k: weight)
        part = jnp.dot(weight, whole[0], preferred_element_type=jnp.float32)
        for k in (1, 2):
            part = part + jnp.dot(got[k], whole[k], preferred_element_type=jnp.float32)
        count = counts[distance - 1] if distance else None
        found, *weight = back_terms(MASKS[distance], part, got[3], whole[3], count, found, word)
        weight = weight[0] if weight else None

    keep, send = spread_found(found)
    pieces = traded(keep, send)
    return brought_home(jnp.concatenate([upper, lower]), pieces)


def solution(mesh):
    placed = (
        P(("row", "col"), None),
        P(("row", "col"), None),
        P(("row", "col"), None),
        P("row", "col", None, None),
        P("row", "col", None, None, None, None),
    )

    def shards(paths_in, dep_in, levels, tile_src, pattern):
        rows, cols = lax.axis_size("row"), lax.axis_size("col")
        fits = (
            rows == 2 * LAYERS
            and 2 * cols == GROUP
            and paths_in.shape[0] == pattern.shape[-1]
            and tile_src.shape[3] == cols
            and paths_in.shape[1] % GROUP == 0
        )
        chosen = split_shards if fits else general_shards
        return chosen(paths_in, dep_in, levels, tile_src, pattern)

    return jax.shard_map(
        shards, mesh=mesh, in_specs=placed, out_specs=P(("row", "col"), None), check_vma=False
    )
```

```python
import functools

import jax
import jax.numpy as jnp
from jax import lax
from jax.experimental import pallas as pl
from jax.experimental.pallas import tpu as pltpu
from jax.sharding import PartitionSpec as P


def general_shards(paths_in, dep_in, levels, tile_src, pattern):
    vert_dev = paths_in.shape[0]
    tile_size = pattern.shape[-1]
    dest_tiles = tile_src.shape[2]
    band_slots = tile_src.shape[3]
    src_tiles = lax.axis_size("col") * vert_dev // tile_size
    per_source = dest_tiles * band_slots // src_tiles
    source_ids = tile_src[0, 0]
    tile_values = pattern[0, 0].astype(jnp.bfloat16)
    flat_ids = source_ids.reshape(-1)
    by_source = jnp.argsort(flat_ids, stable=True)
    back_values = tile_values.reshape(-1, tile_size, tile_size)[by_source]
    back_values = back_values.reshape(src_tiles, per_source, tile_size, tile_size)
    back_dest = (by_source // band_slots).reshape(src_tiles, per_source)

    def forward_terms(frontier):
        gathered = lax.all_gather(frontier, "col", axis=0, tiled=True)
        pieces = gathered.reshape(src_tiles, tile_size, gathered.shape[1])
        product = jnp.einsum(
            "ibrj,ibjs->irs", tile_values, pieces[source_ids], preferred_element_type=jnp.float32
        )
        terms = product.reshape(vert_dev * lax.axis_size("row"), product.shape[2])
        return lax.psum_scatter(terms, "row", scatter_dimension=0, tiled=True)

    def spread(weight):
        return lax.all_gather(weight, "row", axis=0, tiled=True)

    level_masks = [(levels == distance).astype(jnp.float32) for distance in range(4)]
    path_counts = [level_masks[0] * paths_in]
    for distance in (1, 2, 3):
        path_counts.append(
            level_masks[distance] * forward_terms(path_counts[-1].astype(jnp.bfloat16))
        )
    numerator = level_masks[3] * (1.0 + dep_in)
    spread_weight = spread((numerator / jnp.maximum(path_counts[3], 1.0)).astype(jnp.bfloat16))
    dependency = jnp.zeros(paths_in.shape, jnp.float32)
    for distance in (2, 1, 0):
        backward_pieces = spread_weight.reshape(dest_tiles, tile_size, spread_weight.shape[1])
        source_product = jnp.einsum(
            "tgrj,tgrs->tjs",
            back_values,
            backward_pieces[back_dest],
            preferred_element_type=jnp.float32,
        )
        source_product = source_product.reshape(
            vert_dev * lax.axis_size("col"), source_product.shape[2]
        )
        dependence = (
            level_masks[distance]
            * path_counts[distance]
            * lax.psum_scatter(source_product, "col", scatter_dimension=0, tiled=True)
        )
        dependency = dependency + dependence
        if distance > 0:
            weight = (
                level_masks[distance] * (1.0 + dependence) / jnp.maximum(path_counts[distance], 1.0)
            ).astype(jnp.bfloat16)
            spread_weight = spread(weight)
    return dependency


def partner(axis, bit):
    return [(i, i ^ bit) for i in range(lax.axis_size(axis))]


def swap(value, axis, bit):
    return lax.ppermute(value, axis, partner(axis, bit))


def diagonal():
    cols = lax.axis_size("col")
    return [(i, i ^ cols ^ 2) for i in range(lax.axis_size("row") * cols)]


GROUP = 8
LAYERS = 4
SUMS = (3, 1, 2)
SPREADS = (3, 1, 2)
LOWEST = 5
MANTISSA = 18
BYTE = 255


def coded(count):
    scaled = count * 2.0**LOWEST
    exponent = jnp.zeros_like(count)
    for bit in (32, 16, 8, 4, 2, 1):
        large = scaled >= 2.0**bit
        scaled = jnp.where(large, scaled * 2.0**-bit, scaled)
        exponent = exponent + jnp.where(large, float(bit), 0.0)
    mantissa = jnp.floor((scaled - 1.0) * 2.0**MANTISSA + 0.5)
    code = jnp.where(count > 0.0, exponent * 2.0**MANTISSA + mantissa, 0.0).astype(jnp.int32)
    *first, last = jnp.split(code, 4, axis=1)
    words = [part | (((last >> (8 * at)) & BYTE) << 24) for at, part in enumerate(first)]
    return jnp.concatenate(words, axis=1)


def decoded(words):
    words = jnp.split(words, 3, axis=1)
    last = sum(((word >> 24) & BYTE) << (8 * at) for at, word in enumerate(words))
    code = jnp.concatenate([word & (2**24 - 1) for word in words] + [last], axis=1)
    exponent = code >> MANTISSA
    mantissa = code & (2**MANTISSA - 1)
    count = mantissa.astype(jnp.float32) * 2.0 ** (-MANTISSA - LOWEST) + 2.0**-LOWEST
    for bit in (32, 16, 8, 4, 2, 1):
        count = jnp.where((exponent & bit) != 0, count * 2.0**bit, count)
    return jnp.where(code > 0, count, 0.0)


IN_VMEM = pl.BlockSpec(memory_space=pltpu.VMEM)
IN_SMEM = pl.BlockSpec(memory_space=pltpu.SMEM)


def pack_kernel(ids, pattern, *outs):
    cols = outs[0].shape[1]
    row = lax.axis_index("row")
    for layer in reversed(range(LAYERS)):
        for y in range(2):
            i = row ^ (2 * layer + y)
            for t in range(cols):
                slot = jnp.int32(0)
                for e in range(1, cols):
                    slot = jnp.where(ids[e, i] == t, e, slot)
                tile = pattern[i * cols + slot].astype(jnp.float32).astype(jnp.bfloat16)
                if layer:
                    outs[y][layer - 1, t] = tile
                else:
                    outs[2][y, t] = tile
                    outs[3][1 - y, t] = tile


def packed_block(ids, pattern):
    cols, tile = ids.shape[0], pattern.shape[-1]
    other = jax.ShapeDtypeStruct((LAYERS - 1, cols, tile, tile), jnp.bfloat16)
    own = jax.ShapeDtypeStruct((2, cols, tile, tile), jnp.bfloat16)
    return pl.pallas_call(
        pack_kernel,
        out_shape=[other, other, own, own],
        in_specs=[IN_SMEM, IN_VMEM],
        out_specs=[IN_VMEM] * 4,
        compiler_params=pltpu.CompilerParams(vmem_limit_bytes=8 * 1024 * 1024),
        name="pack",
    )(ids, pattern)


def inputs_kernel(paths_in, dep_in, levels, keep, send, words):
    level = levels[...]
    word = jnp.where(
        level == 0, -paths_in[...], jnp.where(level == 3, 1.0 + dep_in[...], 0.0)
    )
    word = jnp.where(level == 1, 0.5, jnp.where(level == 2, 0.25, word))
    words[...] = word.T
    share = keep.shape[-2]
    place = lax.axis_index("row") % 2 * lax.axis_size("col") + lax.axis_index("col")
    for out, core in ((keep, 0), (send, 1)):
        for at in range(GROUP // 2):
            rows = pl.multiple_of((place ^ (2 * at + core)) * share, share)
            out[at] = words[pl.ds(rows, share), :]


def packed_inputs(paths_in, dep_in, levels):
    vert, sources = paths_in.shape
    half = jax.ShapeDtypeStruct((GROUP // 2, sources // GROUP, vert), jnp.float32)
    return pl.pallas_call(
        inputs_kernel,
        out_shape=[half] * 2,
        in_specs=[IN_VMEM] * 3,
        out_specs=[IN_VMEM] * 2,
        scratch_shapes=[pltpu.VMEM((sources, vert), jnp.float32)],
        compiler_params=pltpu.CompilerParams(vmem_limit_bytes=4 * 1024 * 1024),
        name="inputs",
    )(paths_in, dep_in, levels)


def placed_kernel(*rest):
    pieces, word, front = rest[:-2], rest[-2], rest[-1]
    vert = pieces[0].shape[-1]
    col = lax.axis_index("col")
    for at in range(2 * len(pieces)):
        to = (at & 4) | ((at & 3) ^ col)
        piece = pieces[at // 2][at % 2]
        lanes = pl.ds(pl.multiple_of(to * vert, vert), vert)
        word[:, lanes] = piece
        front[:, lanes] = jnp.maximum(-piece, 0.0).astype(jnp.bfloat16)


def placed_inputs(pieces):
    _, share, vert = pieces[0].shape
    shape = (share, 2 * len(pieces) * vert)
    return pl.pallas_call(
        placed_kernel,
        out_shape=[jax.ShapeDtypeStruct(shape, kind) for kind in (jnp.float32, jnp.bfloat16)],
        in_specs=[IN_VMEM] * len(pieces),
        out_specs=[IN_VMEM] * 2,
        compiler_params=pltpu.CompilerParams(vmem_limit_bytes=4 * 1024 * 1024),
        name="placed",
    )(*pieces)


def rows_of(halves, layer):
    cols = halves[0].shape[1]
    return jnp.concatenate(
        [jnp.concatenate([half[layer, t] for t in range(cols)], axis=1) for half in halves], axis=0
    )


def first_kernel(base, front, *rest):
    count = LAYERS - 1
    outs = rest[-count:]
    start = rest[:count] if base else None
    halves = rest[count if base else 0 : -count]
    pairs = ((1, 2), (1, 3)) if base else tuple((at // 4, at % 4) for at in range(6))
    layers, cols, tile, _ = halves[0].shape
    wide = cols * tile
    col = lax.axis_index("col")
    for layer in reversed(range(layers)):
        for flip in range(cols):
            terms = None
            for at, (side, c) in enumerate(pairs):
                if c == flip:
                    term = lax.dot_general(
                        front[:, side * wide : (side + 1) * wide],
                        rows_of(halves[2 * at : 2 * at + 2], layer),
                        (((1,), (1,)), ((), ())),
                        preferred_element_type=jnp.float32,
                    )
                    terms = term if terms is None else terms + term
            for y in range(2):
                lanes = pl.ds(pl.multiple_of((y * cols + (col ^ flip)) * tile, tile), tile)
                if terms is None:
                    outs[layer][:, lanes] = start[layer][:, lanes]
                    continue
                part = terms[:, y * tile : (y + 1) * tile]
                outs[layer][:, lanes] = part + start[layer][:, lanes] if base else part


def first_terms(front, base, halves):
    shape = jax.ShapeDtypeStruct(front.shape, jnp.float32)
    count = LAYERS - 1
    size = len(halves) * halves[0].size
    return pl.pallas_call(
        functools.partial(first_kernel, bool(base)),
        out_shape=[shape] * count,
        in_specs=[IN_VMEM] * (1 + len(base) + len(halves)),
        out_specs=[IN_VMEM] * count,
        compiler_params=pltpu.CompilerParams(vmem_limit_bytes=12 * 1024 * 1024),
        cost_estimate=pl.CostEstimate(
            flops=2 * front.shape[0] * size, bytes_accessed=2 * size, transcendentals=0
        ),
        name="first",
    )(front, *base, *halves)


def assemble_kernel(parts, count, *rest):
    blocks, outs = rest[:count], rest[count:]
    _, cols, tile, _ = blocks[0].shape
    col = lax.axis_index("col")
    for layer, out in enumerate(outs):
        for at in range(count * 2 // parts):
            side, flip, y = at // (2 * cols), at // 2 % cols, at % 2
            block, lead = (blocks[at], layer) if parts == 2 else (blocks[at // 2], y)
            rows = pl.ds(pl.multiple_of((y * cols + (col ^ flip)) * tile, tile), tile)
            for t in range(cols):
                start = (side * cols + t) * tile
                out[rows, start : start + tile] = block[lead, t]


def assembled(blocks, parts):
    lead, cols, tile, _ = blocks[0].shape
    span = 2 * cols * tile
    layers = lead if parts == 2 else 1
    return pl.pallas_call(
        functools.partial(assemble_kernel, parts, len(blocks)),
        out_shape=[jax.ShapeDtypeStruct((span, span), jnp.bfloat16)] * layers,
        in_specs=[IN_VMEM] * len(blocks),
        out_specs=[IN_VMEM] * layers,
        compiler_params=pltpu.CompilerParams(vmem_limit_bytes=16 * 1024 * 1024),
        cost_estimate=pl.CostEstimate(
            flops=0, bytes_accessed=4 * len(blocks) * blocks[0].size, transcendentals=0
        ),
        name="assemble",
    )(*blocks)


def lead_kernel(mask, own, *rest):
    got, word, whole, count, front, words = rest[:-5], rest[-5], rest[-4], rest[-3], rest[-2], rest[-1]
    total = own[...]
    for message in got:
        total = total + decoded(message[...])
    total = jnp.where(mask(word[...]), total, 0.0)
    count[...] = total
    front[...] = total.astype(jnp.bfloat16)
    words[...] = coded(across_terms(front[...], whole[...]))


def across_terms(front, whole):
    return lax.dot_general(
        front, whole, (((1,), (1,)), ((), ())), preferred_element_type=jnp.float32
    )


def message_kernel(front, whole, words):
    words[...] = coded(across_terms(front[...], whole[...]))


def vmem_call(kernel, outs, args, flops):
    moved = sum(x.size * x.dtype.itemsize for x in (*outs, *args))
    return pl.pallas_call(
        kernel,
        out_shape=outs,
        in_specs=[IN_VMEM] * len(args),
        out_specs=[IN_VMEM] * len(outs),
        compiler_params=pltpu.CompilerParams(vmem_limit_bytes=8 * 1024 * 1024),
        cost_estimate=pl.CostEstimate(flops=flops, bytes_accessed=moved, transcendentals=0),
    )(*args)


def level_terms(mask, own, got, word, whole):
    share, span = own.shape
    outs = [
        jax.ShapeDtypeStruct((share, span), jnp.float32),
        jax.ShapeDtypeStruct((share, span), jnp.bfloat16),
        jax.ShapeDtypeStruct((share, span // 4 * 3), jnp.int32),
    ]
    flops = 2 * share * whole.size
    return vmem_call(functools.partial(lead_kernel, mask), outs, [own, *got, word, whole], flops)


def message(front, whole):
    share, span = front.shape
    outs = [jax.ShapeDtypeStruct((share, span // 4 * 3), jnp.int32)]
    return vmem_call(message_kernel, outs, [front, whole], 2 * share * whole.size)[0]


def back_kernel(mask, last, part, weight, whole, *rest):
    out = rest[-1]
    back = part[...] + jnp.dot(weight[...], whole[...], preferred_element_type=jnp.float32)
    if last:
        found, word = rest[0], rest[1]
        out[...] = found[...] + jnp.where(mask(word[...]), back, 0.0)
        return
    count, found, word, grown = rest[0], rest[1], rest[2], rest[3]
    delta = count[...] * back
    grown[...] = found[...] + delta
    new = jnp.where(mask(word[...]), (1.0 + delta) / jnp.maximum(count[...], 1.0), 0.0)
    out[...] = new.astype(jnp.bfloat16)


def back_terms(mask, part, weight, whole, count, found, word):
    last = count is None
    outs = [jax.ShapeDtypeStruct(found.shape, jnp.float32)]
    if not last:
        outs.append(jax.ShapeDtypeStruct(found.shape, jnp.bfloat16))
    args = [part, weight, whole] + ([] if last else [count]) + [found, word]
    flops = 2 * found.shape[0] * whole.size
    return vmem_call(functools.partial(back_kernel, mask, last), outs, args, flops)


MASKS = (
    lambda word: word < 0.0,
    lambda word: word == 0.5,
    lambda word: word == 0.25,
    lambda word: word >= 1.0,
)


def spread_kernel(found, keep, send):
    place = lax.axis_index("row") % 2 * lax.axis_size("col") + lax.axis_index("col")
    vert = keep.shape[-1]
    cols = lax.axis_size("col")
    for out, core in ((keep, 0), (send, 1)):
        for at in range(GROUP // 2):
            rel = 2 * at + core
            to = (rel & cols) | ((rel & (cols - 1)) ^ (place & (cols - 1)))
            out[at] = found[:, pl.ds(pl.multiple_of(to * vert, vert), vert)]


def spread_found(found):
    share, span = found.shape
    half = jax.ShapeDtypeStruct((GROUP // 2, share, span // GROUP), jnp.float32)
    return pl.pallas_call(
        spread_kernel,
        out_shape=[half] * 2,
        in_specs=[IN_VMEM],
        out_specs=[IN_VMEM] * 2,
        compiler_params=pltpu.CompilerParams(vmem_limit_bytes=4 * 1024 * 1024),
        name="spread",
    )(found)


def home_kernel(factor, *rest):
    pieces, out, words = rest[:-2], rest[-2], rest[-1]
    place = lax.axis_index("row") % 2 * lax.axis_size("col") + lax.axis_index("col")
    share = pieces[0].shape[-2]
    for at in range(2 * len(pieces)):
        rows = pl.multiple_of((place ^ at) * share, share)
        words[pl.ds(rows, share), :] = pieces[at // 2][at % 2]
    out[...] = words[...].T * factor[...]


def brought_home(factor, pieces):
    vert, sources = factor.shape
    return pl.pallas_call(
        home_kernel,
        out_shape=jax.ShapeDtypeStruct((vert, sources), jnp.float32),
        in_specs=[IN_VMEM] * (1 + len(pieces)),
        out_specs=IN_VMEM,
        scratch_shapes=[pltpu.VMEM((sources, vert), jnp.float32)],
        compiler_params=pltpu.CompilerParams(vmem_limit_bytes=4 * 1024 * 1024),
        name="home",
    )(factor, *pieces)


def traded(keep, send):
    got = swap(send, "col", 1)
    held = [jnp.stack([keep[at], got[at]]) for at in range(GROUP // 2)]
    from_y = swap(held[2], "row", 1)
    from_x = swap(held[1], "col", 2)
    from_d = lax.ppermute(held[3], ("row", "col"), diagonal())
    return [held[0], from_x, from_y, from_d]


def split_shards(paths_in, dep_in, levels, tile_src, pattern):
    vert, _ = paths_in.shape
    tile = pattern.shape[-1]

    *own, same, flipped = packed_block(tile_src[0, 0].T, pattern[0, 0].reshape(-1, tile, tile))
    keep, send = packed_inputs(paths_in, dep_in, levels)
    pieces = traded(keep, send)
    by_y = [swap(own[1], "row", 1)]
    by_x = [swap(own[0], "col", 2)]
    by_core = [swap(half, "col", 1) for half in own]
    by_y.append(swap(own[0], "row", 1))
    by_x.append(swap(own[1], "col", 2))

    upper = jnp.where(levels == 0, paths_in, 1.0)[: vert // 2]
    lower = jnp.where(levels == 0, paths_in, 1.0)[vert // 2 :]
    upper, lower = lax.optimization_barrier((upper, lower))

    word, front = placed_inputs(pieces)
    cross = [swap(by_y[0], "col", 2), swap(by_x[0], "row", 1)]
    same_y = swap(flipped, "row", 1)
    same_x = swap(same, "col", 2)
    same_d = lax.ppermute(flipped, ("row", "col"), diagonal())
    crossed = [swap(by_x[0], "col", 1), swap(by_y[0], "col", 1)]
    crossed += [swap(by_x[1], "col", 1), swap(by_y[1], "col", 1)]
    near = list(own) + by_core + by_x + [crossed[0], crossed[2]]
    far = by_y + [crossed[1], crossed[3]]
    last = cross + [swap(half, "col", 1) for half in cross]
    first = first_terms(front, [], near + far)
    first = first_terms(front, first, last)
    blocks = [
        part
        for block in (same, same_x, same_y, same_d)
        for part in (block, swap(block, "col", 1))
    ]
    others = assembled(near + far + last, 2)
    whole = assembled(blocks, 1) + others

    def across(order, value):
        got = {}
        for k in order:
            got[k] = swap(value(k), "row", 2 * k)
        return got

    got = across(SUMS, lambda k: coded(first[k - 1]))
    counts = []
    for distance in (1, 2):
        own = across_terms(front, whole[0])
        got = [got[k] for k in range(1, LAYERS)]
        count, front, words = level_terms(MASKS[distance], own, got, word, whole[SUMS[0]])
        counts.append(count)
        got = across(SUMS, lambda k: words if k == SUMS[0] else message(front, whole[k]))
    total = across_terms(front, whole[0])
    for k in range(1, LAYERS):
        total = total + decoded(got[k])
    weight = jnp.where(MASKS[3](word), word / jnp.maximum(total, 1.0), 0.0).astype(jnp.bfloat16)
    found = jnp.zeros_like(word)
    for distance in (2, 1, 0):
        got = across(SPREADS, lambda k: weight)
        part = jnp.dot(weight, whole[0], preferred_element_type=jnp.float32)
        for k in SPREADS[:-1]:
            part = part + jnp.dot(got[k], whole[k], preferred_element_type=jnp.float32)
        count = counts[distance - 1] if distance else None
        found, *weight = back_terms(MASKS[distance], part, got[SPREADS[-1]], whole[SPREADS[-1]], count, found, word)
        weight = weight[0] if weight else None

    keep, send = spread_found(found)
    pieces = traded(keep, send)
    return brought_home(jnp.concatenate([upper, lower]), pieces)


def solution(mesh):
    placed = (
        P(("row", "col"), None),
        P(("row", "col"), None),
        P(("row", "col"), None),
        P("row", "col", None, None),
        P("row", "col", None, None, None, None),
    )

    def shards(paths_in, dep_in, levels, tile_src, pattern):
        rows, cols = lax.axis_size("row"), lax.axis_size("col")
        fits = (
            rows == 2 * LAYERS
            and 2 * cols == GROUP
            and paths_in.shape[0] == pattern.shape[-1]
            and tile_src.shape[3] == cols
            and paths_in.shape[1] % GROUP == 0
        )
        chosen = split_shards if fits else general_shards
        return chosen(paths_in, dep_in, levels, tile_src, pattern)

    return jax.shard_map(
        shards, mesh=mesh, in_specs=placed, out_specs=P(("row", "col"), None), check_vma=False
    )
```

```python
import functools

import jax
import jax.numpy as jnp
from jax import lax
from jax.experimental import pallas as pl
from jax.experimental.pallas import tpu as pltpu
from jax.sharding import PartitionSpec as P


def general_shards(paths_in, dep_in, levels, tile_src, pattern):
    vert_dev = paths_in.shape[0]
    tile_size = pattern.shape[-1]
    dest_tiles = tile_src.shape[2]
    band_slots = tile_src.shape[3]
    src_tiles = lax.axis_size("col") * vert_dev // tile_size
    per_source = dest_tiles * band_slots // src_tiles
    source_ids = tile_src[0, 0]
    tile_values = pattern[0, 0].astype(jnp.bfloat16)
    flat_ids = source_ids.reshape(-1)
    by_source = jnp.argsort(flat_ids, stable=True)
    back_values = tile_values.reshape(-1, tile_size, tile_size)[by_source]
    back_values = back_values.reshape(src_tiles, per_source, tile_size, tile_size)
    back_dest = (by_source // band_slots).reshape(src_tiles, per_source)

    def forward_terms(frontier):
        gathered = lax.all_gather(frontier, "col", axis=0, tiled=True)
        pieces = gathered.reshape(src_tiles, tile_size, gathered.shape[1])
        product = jnp.einsum(
            "ibrj,ibjs->irs", tile_values, pieces[source_ids], preferred_element_type=jnp.float32
        )
        terms = product.reshape(vert_dev * lax.axis_size("row"), product.shape[2])
        return lax.psum_scatter(terms, "row", scatter_dimension=0, tiled=True)

    def spread(weight):
        return lax.all_gather(weight, "row", axis=0, tiled=True)

    level_masks = [(levels == distance).astype(jnp.float32) for distance in range(4)]
    path_counts = [level_masks[0] * paths_in]
    for distance in (1, 2, 3):
        path_counts.append(
            level_masks[distance] * forward_terms(path_counts[-1].astype(jnp.bfloat16))
        )
    numerator = level_masks[3] * (1.0 + dep_in)
    spread_weight = spread((numerator / jnp.maximum(path_counts[3], 1.0)).astype(jnp.bfloat16))
    dependency = jnp.zeros(paths_in.shape, jnp.float32)
    for distance in (2, 1, 0):
        backward_pieces = spread_weight.reshape(dest_tiles, tile_size, spread_weight.shape[1])
        source_product = jnp.einsum(
            "tgrj,tgrs->tjs",
            back_values,
            backward_pieces[back_dest],
            preferred_element_type=jnp.float32,
        )
        source_product = source_product.reshape(
            vert_dev * lax.axis_size("col"), source_product.shape[2]
        )
        dependence = (
            level_masks[distance]
            * path_counts[distance]
            * lax.psum_scatter(source_product, "col", scatter_dimension=0, tiled=True)
        )
        dependency = dependency + dependence
        if distance > 0:
            weight = (
                level_masks[distance] * (1.0 + dependence) / jnp.maximum(path_counts[distance], 1.0)
            ).astype(jnp.bfloat16)
            spread_weight = spread(weight)
    return dependency


def partner(axis, bit):
    return [(i, i ^ bit) for i in range(lax.axis_size(axis))]


def swap(value, axis, bit):
    return lax.ppermute(value, axis, partner(axis, bit))


def diagonal():
    cols = lax.axis_size("col")
    return [(i, i ^ cols ^ 2) for i in range(lax.axis_size("row") * cols)]


GROUP = 8
LAYERS = 4
SUMS = (3, 1, 2)
SPREADS = (3, 1, 2)
LOWEST = 5
MANTISSA = 18
BYTE = 255


def coded(count):
    scaled = count * 2.0**LOWEST
    exponent = jnp.zeros_like(count)
    for bit in (32, 16, 8, 4, 2, 1):
        large = scaled >= 2.0**bit
        scaled = jnp.where(large, scaled * 2.0**-bit, scaled)
        exponent = exponent + jnp.where(large, float(bit), 0.0)
    mantissa = jnp.floor((scaled - 1.0) * 2.0**MANTISSA + 0.5)
    code = jnp.where(count > 0.0, exponent * 2.0**MANTISSA + mantissa, 0.0).astype(jnp.int32)
    *first, last = jnp.split(code, 4, axis=1)
    words = [part | (((last >> (8 * at)) & BYTE) << 24) for at, part in enumerate(first)]
    return jnp.concatenate(words, axis=1)


def decoded(words):
    words = jnp.split(words, 3, axis=1)
    last = sum(((word >> 24) & BYTE) << (8 * at) for at, word in enumerate(words))
    code = jnp.concatenate([word & (2**24 - 1) for word in words] + [last], axis=1)
    exponent = code >> MANTISSA
    mantissa = code & (2**MANTISSA - 1)
    count = mantissa.astype(jnp.float32) * 2.0 ** (-MANTISSA - LOWEST) + 2.0**-LOWEST
    for bit in (32, 16, 8, 4, 2, 1):
        count = jnp.where((exponent & bit) != 0, count * 2.0**bit, count)
    return jnp.where(code > 0, count, 0.0)


IN_VMEM = pl.BlockSpec(memory_space=pltpu.VMEM)
IN_SMEM = pl.BlockSpec(memory_space=pltpu.SMEM)


def pack_kernel(ids, pattern, *outs):
    cols = outs[0].shape[1]
    row = lax.axis_index("row")
    for layer in reversed(range(LAYERS)):
        for y in range(2):
            i = row ^ (2 * layer + y)
            for t in range(cols):
                slot = jnp.int32(0)
                for e in range(1, cols):
                    slot = jnp.where(ids[e, i] == t, e, slot)
                tile = pattern[i * cols + slot].astype(jnp.float32).astype(jnp.bfloat16)
                if layer:
                    outs[y][layer - 1, t] = tile
                else:
                    outs[2][y, t] = tile
                    outs[3][1 - y, t] = tile


def packed_block(ids, pattern):
    cols, tile = ids.shape[0], pattern.shape[-1]
    other = jax.ShapeDtypeStruct((LAYERS - 1, cols, tile, tile), jnp.bfloat16)
    own = jax.ShapeDtypeStruct((2, cols, tile, tile), jnp.bfloat16)
    return pl.pallas_call(
        pack_kernel,
        out_shape=[other, other, own, own],
        in_specs=[IN_SMEM, IN_VMEM],
        out_specs=[IN_VMEM] * 4,
        compiler_params=pltpu.CompilerParams(vmem_limit_bytes=8 * 1024 * 1024),
        name="pack",
    )(ids, pattern)


def inputs_kernel(paths_in, dep_in, levels, keep, send, words):
    level = levels[...]
    word = jnp.where(
        level == 0, -paths_in[...], jnp.where(level == 3, 1.0 + dep_in[...], 0.0)
    )
    word = jnp.where(level == 1, 0.5, jnp.where(level == 2, 0.25, word))
    words[...] = word.T
    share = keep.shape[-2]
    place = lax.axis_index("row") % 2 * lax.axis_size("col") + lax.axis_index("col")
    for out, core in ((keep, 0), (send, 1)):
        for at in range(GROUP // 2):
            rows = pl.multiple_of((place ^ (2 * at + core)) * share, share)
            out[at] = words[pl.ds(rows, share), :]


def packed_inputs(paths_in, dep_in, levels):
    vert, sources = paths_in.shape
    half = jax.ShapeDtypeStruct((GROUP // 2, sources // GROUP, vert), jnp.float32)
    return pl.pallas_call(
        inputs_kernel,
        out_shape=[half] * 2,
        in_specs=[IN_VMEM] * 3,
        out_specs=[IN_VMEM] * 2,
        scratch_shapes=[pltpu.VMEM((sources, vert), jnp.float32)],
        compiler_params=pltpu.CompilerParams(vmem_limit_bytes=4 * 1024 * 1024),
        name="inputs",
    )(paths_in, dep_in, levels)


def placed_kernel(*rest):
    pieces, word, front = rest[:-2], rest[-2], rest[-1]
    vert = pieces[0].shape[-1]
    col = lax.axis_index("col")
    for at in range(2 * len(pieces)):
        to = (at & 4) | ((at & 3) ^ col)
        piece = pieces[at // 2][at % 2]
        lanes = pl.ds(pl.multiple_of(to * vert, vert), vert)
        word[:, lanes] = piece
        front[:, lanes] = jnp.maximum(-piece, 0.0).astype(jnp.bfloat16)


def placed_inputs(pieces):
    _, share, vert = pieces[0].shape
    shape = (share, 2 * len(pieces) * vert)
    return pl.pallas_call(
        placed_kernel,
        out_shape=[jax.ShapeDtypeStruct(shape, kind) for kind in (jnp.float32, jnp.bfloat16)],
        in_specs=[IN_VMEM] * len(pieces),
        out_specs=[IN_VMEM] * 2,
        compiler_params=pltpu.CompilerParams(vmem_limit_bytes=4 * 1024 * 1024),
        name="placed",
    )(*pieces)


def rows_of(halves, layer):
    cols = halves[0].shape[1]
    return jnp.concatenate(
        [jnp.concatenate([half[layer, t] for t in range(cols)], axis=1) for half in halves], axis=0
    )


def first_kernel(base, front, *rest):
    count = LAYERS - 1
    outs = rest[-count:]
    start = rest[:count] if base else None
    halves = rest[count if base else 0 : -count]
    pairs = ((1, 2), (1, 3)) if base else tuple((at // 4, at % 4) for at in range(6))
    layers, cols, tile, _ = halves[0].shape
    wide = cols * tile
    col = lax.axis_index("col")
    for layer in reversed(range(layers)):
        for flip in range(cols):
            terms = None
            for at, (side, c) in enumerate(pairs):
                if c == flip:
                    term = lax.dot_general(
                        front[:, side * wide : (side + 1) * wide],
                        rows_of(halves[2 * at : 2 * at + 2], layer),
                        (((1,), (1,)), ((), ())),
                        preferred_element_type=jnp.float32,
                    )
                    terms = term if terms is None else terms + term
            for y in range(2):
                lanes = pl.ds(pl.multiple_of((y * cols + (col ^ flip)) * tile, tile), tile)
                if terms is None:
                    outs[layer][:, lanes] = start[layer][:, lanes]
                    continue
                part = terms[:, y * tile : (y + 1) * tile]
                outs[layer][:, lanes] = part + start[layer][:, lanes] if base else part


def first_terms(front, base, halves):
    shape = jax.ShapeDtypeStruct(front.shape, jnp.float32)
    count = LAYERS - 1
    size = len(halves) * halves[0].size
    return pl.pallas_call(
        functools.partial(first_kernel, bool(base)),
        out_shape=[shape] * count,
        in_specs=[IN_VMEM] * (1 + len(base) + len(halves)),
        out_specs=[IN_VMEM] * count,
        compiler_params=pltpu.CompilerParams(vmem_limit_bytes=12 * 1024 * 1024),
        cost_estimate=pl.CostEstimate(
            flops=2 * front.shape[0] * size, bytes_accessed=2 * size, transcendentals=0
        ),
        name="first",
    )(front, *base, *halves)


def assemble_kernel(parts, count, *rest):
    blocks, outs = rest[:count], rest[count:]
    _, cols, tile, _ = blocks[0].shape
    col = lax.axis_index("col")
    for layer, out in enumerate(outs):
        for at in range(count * 2 // parts):
            side, flip, y = at // (2 * cols), at // 2 % cols, at % 2
            block, lead = (blocks[at], layer) if parts == 2 else (blocks[at // 2], y)
            rows = pl.ds(pl.multiple_of((y * cols + (col ^ flip)) * tile, tile), tile)
            for t in range(cols):
                start = (side * cols + t) * tile
                out[rows, start : start + tile] = block[lead, t]


def assembled(blocks, parts):
    lead, cols, tile, _ = blocks[0].shape
    span = 2 * cols * tile
    layers = lead if parts == 2 else 1
    return pl.pallas_call(
        functools.partial(assemble_kernel, parts, len(blocks)),
        out_shape=[jax.ShapeDtypeStruct((span, span), jnp.bfloat16)] * layers,
        in_specs=[IN_VMEM] * len(blocks),
        out_specs=[IN_VMEM] * layers,
        compiler_params=pltpu.CompilerParams(vmem_limit_bytes=16 * 1024 * 1024),
        cost_estimate=pl.CostEstimate(
            flops=0, bytes_accessed=4 * len(blocks) * blocks[0].size, transcendentals=0
        ),
        name="assemble",
    )(*blocks)


def lead_kernel(mask, own, *rest):
    got, word, whole, count, front, words = rest[:-5], rest[-5], rest[-4], rest[-3], rest[-2], rest[-1]
    total = own[...]
    for message in got:
        total = total + decoded(message[...])
    total = jnp.where(mask(word[...]), total, 0.0)
    count[...] = total
    front[...] = total.astype(jnp.bfloat16)
    words[...] = coded(across_terms(front[...], whole[...]))


def across_terms(front, whole):
    return lax.dot_general(
        front, whole, (((1,), (1,)), ((), ())), preferred_element_type=jnp.float32
    )


def message_kernel(front, whole, words):
    words[...] = coded(across_terms(front[...], whole[...]))


def vmem_call(kernel, outs, args, flops):
    moved = sum(x.size * x.dtype.itemsize for x in (*outs, *args))
    return pl.pallas_call(
        kernel,
        out_shape=outs,
        in_specs=[IN_VMEM] * len(args),
        out_specs=[IN_VMEM] * len(outs),
        compiler_params=pltpu.CompilerParams(vmem_limit_bytes=8 * 1024 * 1024),
        cost_estimate=pl.CostEstimate(flops=flops, bytes_accessed=moved, transcendentals=0),
    )(*args)


def level_terms(mask, own, got, word, whole):
    share, span = own.shape
    outs = [
        jax.ShapeDtypeStruct((share, span), jnp.float32),
        jax.ShapeDtypeStruct((share, span), jnp.bfloat16),
        jax.ShapeDtypeStruct((share, span // 4 * 3), jnp.int32),
    ]
    flops = 2 * share * whole.size
    return vmem_call(functools.partial(lead_kernel, mask), outs, [own, *got, word, whole], flops)


def message(front, whole):
    share, span = front.shape
    outs = [jax.ShapeDtypeStruct((share, span // 4 * 3), jnp.int32)]
    return vmem_call(message_kernel, outs, [front, whole], 2 * share * whole.size)[0]


def back_kernel(mask, last, part, weight, whole, *rest):
    out = rest[-1]
    back = part[...] + jnp.dot(weight[...], whole[...], preferred_element_type=jnp.float32)
    if last:
        found, word = rest[0], rest[1]
        out[...] = found[...] + jnp.where(mask(word[...]), back, 0.0)
        return
    count, found, word, grown = rest[0], rest[1], rest[2], rest[3]
    delta = count[...] * back
    grown[...] = found[...] + delta
    new = jnp.where(mask(word[...]), (1.0 + delta) / jnp.maximum(count[...], 1.0), 0.0)
    out[...] = new.astype(jnp.bfloat16)


def back_terms(mask, part, weight, whole, count, found, word):
    last = count is None
    outs = [jax.ShapeDtypeStruct(found.shape, jnp.float32)]
    if not last:
        outs.append(jax.ShapeDtypeStruct(found.shape, jnp.bfloat16))
    args = [part, weight, whole] + ([] if last else [count]) + [found, word]
    flops = 2 * found.shape[0] * whole.size
    return vmem_call(functools.partial(back_kernel, mask, last), outs, args, flops)


MASKS = (
    lambda word: word < 0.0,
    lambda word: word == 0.5,
    lambda word: word == 0.25,
    lambda word: word >= 1.0,
)


def spread_kernel(found, keep, send):
    place = lax.axis_index("row") % 2 * lax.axis_size("col") + lax.axis_index("col")
    vert = keep.shape[-1]
    cols = lax.axis_size("col")
    for out, core in ((keep, 0), (send, 1)):
        for at in range(GROUP // 2):
            rel = 2 * at + core
            to = (rel & cols) | ((rel & (cols - 1)) ^ (place & (cols - 1)))
            out[at] = found[:, pl.ds(pl.multiple_of(to * vert, vert), vert)]


def spread_found(found):
    share, span = found.shape
    half = jax.ShapeDtypeStruct((GROUP // 2, share, span // GROUP), jnp.float32)
    return pl.pallas_call(
        spread_kernel,
        out_shape=[half] * 2,
        in_specs=[IN_VMEM],
        out_specs=[IN_VMEM] * 2,
        compiler_params=pltpu.CompilerParams(vmem_limit_bytes=4 * 1024 * 1024),
        name="spread",
    )(found)


def home_kernel(factor, *rest):
    pieces, out, words = rest[:-2], rest[-2], rest[-1]
    place = lax.axis_index("row") % 2 * lax.axis_size("col") + lax.axis_index("col")
    share = pieces[0].shape[-2]
    for at in range(2 * len(pieces)):
        rows = pl.multiple_of((place ^ at) * share, share)
        words[pl.ds(rows, share), :] = pieces[at // 2][at % 2]
    out[...] = words[...].T * factor[...]


def brought_home(factor, pieces):
    vert, sources = factor.shape
    return pl.pallas_call(
        home_kernel,
        out_shape=jax.ShapeDtypeStruct((vert, sources), jnp.float32),
        in_specs=[IN_VMEM] * (1 + len(pieces)),
        out_specs=IN_VMEM,
        scratch_shapes=[pltpu.VMEM((sources, vert), jnp.float32)],
        compiler_params=pltpu.CompilerParams(vmem_limit_bytes=4 * 1024 * 1024),
        name="home",
    )(factor, *pieces)


def stack_kernel(keep, got, *outs):
    for at, out in enumerate(outs):
        out[0] = keep[at]
        out[1] = got[at]


def stacked(keep, got):
    pair = jax.ShapeDtypeStruct((2, *keep.shape[1:]), keep.dtype)
    return vmem_call(stack_kernel, [pair] * (GROUP // 2), [keep, got], 0)


def traded(keep, send):
    got = swap(send, "col", 1)
    held = stacked(keep, got)
    from_y = swap(held[2], "row", 1)
    from_x = swap(held[1], "col", 2)
    from_d = lax.ppermute(held[3], ("row", "col"), diagonal())
    return [held[0], from_x, from_y, from_d]


def split_shards(paths_in, dep_in, levels, tile_src, pattern):
    vert, _ = paths_in.shape
    tile = pattern.shape[-1]

    *own, same, flipped = packed_block(tile_src[0, 0].T, pattern[0, 0].reshape(-1, tile, tile))
    keep, send = packed_inputs(paths_in, dep_in, levels)
    pieces = traded(keep, send)
    by_y = [swap(own[1], "row", 1)]
    by_x = [swap(own[0], "col", 2)]
    by_core = [swap(half, "col", 1) for half in own]
    by_y.append(swap(own[0], "row", 1))
    by_x.append(swap(own[1], "col", 2))

    upper = jnp.where(levels == 0, paths_in, 1.0)[: vert // 2]
    lower = jnp.where(levels == 0, paths_in, 1.0)[vert // 2 :]
    upper, lower = lax.optimization_barrier((upper, lower))

    word, front = placed_inputs(pieces)
    cross = [swap(by_y[0], "col", 2), swap(by_x[0], "row", 1)]
    same_y = swap(flipped, "row", 1)
    same_x = swap(same, "col", 2)
    same_d = lax.ppermute(flipped, ("row", "col"), diagonal())
    crossed = [swap(by_x[0], "col", 1), swap(by_y[0], "col", 1)]
    crossed += [swap(by_x[1], "col", 1), swap(by_y[1], "col", 1)]
    near = list(own) + by_core + by_x + [crossed[0], crossed[2]]
    far = by_y + [crossed[1], crossed[3]]
    last = cross + [swap(half, "col", 1) for half in cross]
    first = first_terms(front, [], near + far)
    first = first_terms(front, first, last)
    blocks = [
        part
        for block in (same, same_x, same_y, same_d)
        for part in (block, swap(block, "col", 1))
    ]
    others = assembled(near + far + last, 2)
    whole = assembled(blocks, 1) + others

    def across(order, value):
        got = {}
        for k in order:
            got[k] = swap(value(k), "row", 2 * k)
        return got

    got = across(SUMS, lambda k: coded(first[k - 1]))
    counts = []
    for distance in (1, 2):
        own = across_terms(front, whole[0])
        got = [got[k] for k in range(1, LAYERS)]
        count, front, words = level_terms(MASKS[distance], own, got, word, whole[SUMS[0]])
        counts.append(count)
        got = across(SUMS, lambda k: words if k == SUMS[0] else message(front, whole[k]))
    total = across_terms(front, whole[0])
    for k in range(1, LAYERS):
        total = total + decoded(got[k])
    weight = jnp.where(MASKS[3](word), word / jnp.maximum(total, 1.0), 0.0).astype(jnp.bfloat16)
    found = jnp.zeros_like(word)
    for distance in (2, 1, 0):
        got = across(SPREADS, lambda k: weight)
        part = jnp.dot(weight, whole[0], preferred_element_type=jnp.float32)
        for k in SPREADS[:-1]:
            part = part + jnp.dot(got[k], whole[k], preferred_element_type=jnp.float32)
        count = counts[distance - 1] if distance else None
        found, *weight = back_terms(MASKS[distance], part, got[SPREADS[-1]], whole[SPREADS[-1]], count, found, word)
        weight = weight[0] if weight else None

    keep, send = spread_found(found)
    pieces = traded(keep, send)
    return brought_home(jnp.concatenate([upper, lower]), pieces)


def solution(mesh):
    placed = (
        P(("row", "col"), None),
        P(("row", "col"), None),
        P(("row", "col"), None),
        P("row", "col", None, None),
        P("row", "col", None, None, None, None),
    )

    def shards(paths_in, dep_in, levels, tile_src, pattern):
        rows, cols = lax.axis_size("row"), lax.axis_size("col")
        fits = (
            rows == 2 * LAYERS
            and 2 * cols == GROUP
            and paths_in.shape[0] == pattern.shape[-1]
            and tile_src.shape[3] == cols
            and paths_in.shape[1] % GROUP == 0
        )
        chosen = split_shards if fits else general_shards
        return chosen(paths_in, dep_in, levels, tile_src, pattern)

    return jax.shard_map(
        shards, mesh=mesh, in_specs=placed, out_specs=P(("row", "col"), None), check_vma=False
    )
```
